32 devices in a mesh: groups: 2 (over y), filt: 4 (over z), sp: 2 (over x), in: 2 (over core).
Axes of the slice: x: 2, y: 2, z: 4, core: 2. Of those that a mesh axis runs over, the one named last changes fastest.
Arguments:
- image: bfloat16 [16, 256, 1024], P(('groups', 'sp', 'filt'), None, 'in'), parts along dimension 0, may hold values from -6 to 6
- weight: bfloat16 [3, 3, 1024, 1024], P(None, None, 'filt'), may hold values from -0.0625 to 0.0625
- bias: float32 [1024], P('filt'), may hold values from -3 to 3
- cotangent: bfloat16 [16, 1024, 256], P(('groups', 'sp'), 'filt'), parts along dimension 0, may hold values from -0.029907227 to 0.029907227
Outputs:
- output: bfloat16 [16, 1024, 256], P(('groups', 'sp', 'filt'), None, 'in'), parts along dimension 0
- grad_weight: float32 [6, 3, 1024, 1024], P('groups', None, 'filt', 'in'), parts along dimension 0
- grad_bias: float32 [2048], P(('groups', 'filt')), parts along dimension 0
The draws below stay inside these ranges and needn't reach their ends.
There are 2 independent parts, one for each index of `groups`. The reference program is written for one: setup_inputs(seed, part) draws one part's arguments, and reference() takes and returns one part's arrays. A program takes and returns all parts, laid end to end along the dimension named above; an argument that names none is the same for every part. Nothing has to cross between parts.
All inputs are finite; a program needn't handle non-finite values.
Results may differ from the reference program's by a relative error of at most 0.0055.
Values may be sent and summed in bfloat16 or wider, within the bound.
A program may use at most 64 MiB of HBM per device.

```python
import jax
import jax.numpy as jnp

CH = 1024
ROWS_DEV = 1
COLS = 256
ROWS = 8
N_FILT = 4
N_SP = 2


def shard_levels(own_key, dims, cuts, least, largest):
    def one(axis_at, shards_of):
        draws = jax.random.uniform(jax.random.fold_in(jax.random.fold_in(own_key, 6), axis_at), (shards_of,), jnp.float32, least / len(cuts), largest / len(cuts))
        return jnp.repeat(jnp.exp(draws), dims[axis_at] // shards_of).reshape((-1,) + (1,) * (len(dims) - axis_at - 1))

    level = one(*cuts[0])
    for cut in cuts[1:]:
        level = level * one(*cut)
    return level


def noise(key, dims, deviation, most, cuts=(), dtype=jnp.bfloat16):
    array = deviation * jax.random.normal(key, dims, jnp.float32)
    if cuts:
        array = array * shard_levels(key, dims, cuts, -0.22, 0.18)
    return jnp.clip(array, -most, most).astype(dtype)


def setup_inputs(seed: int = 0, part: int = 0) -> dict:
    key_of = jax.random.split(jax.random.key(seed), 5)
    part_keys = jax.random.split(jax.random.fold_in(key_of[4], part), 5)
    image = noise(part_keys[0], (ROWS, COLS, CH), 1.0, 6.0, ((0, 8), (2, 2)))
    weight = noise(key_of[1], (3, 3, CH, CH), (9 * CH) ** -0.5, 0.0625, ((2, 4),))
    bias = noise(key_of[2], (CH,), 0.5, 3.0, ((0, 4),), jnp.float32)
    cotangent = noise(part_keys[3], (ROWS, CH, COLS), 0.005, 0.029907227, ((0, 2), (1, 4)))
    return {"image": image, "weight": weight, "bias": bias, "cotangent": cotangent}


def reference(image, weight, bias, cotangent):
    row_count = ROWS_DEV * N_FILT * N_SP
    col_count = COLS
    padded = jnp.pad(image, ((1, 1), (1, 1), (0, 0)))
    running = jnp.zeros((row_count * col_count, CH), jnp.float32)
    for row_tap in range(3):
        for col_tap in range(3):
            window = padded[row_tap:row_tap + row_count, col_tap:col_tap + col_count].reshape(-1, CH)
            running = running + jnp.dot(window, weight[row_tap, col_tap].T, preferred_element_type=jnp.float32)
    shifted = running + bias[None, :]
    sigmoid_v = jax.nn.sigmoid(shifted)
    output = (shifted * sigmoid_v).astype(jnp.bfloat16).reshape(row_count, col_count, CH).transpose(0, 2, 1)
    slope = sigmoid_v * (1.0 + shifted * (1.0 - sigmoid_v))
    cot_rows = cotangent.transpose(0, 2, 1).reshape(-1, CH)
    grad_out = (cot_rows.astype(jnp.float32) * slope).astype(jnp.bfloat16)
    pieces = []
    for row_tap in range(3):
        for col_tap in range(3):
            window = padded[row_tap:row_tap + row_count, col_tap:col_tap + col_count].reshape(-1, CH)
            pieces.append(jnp.dot(grad_out.T, window, preferred_element_type=jnp.float32))
    grad_weight = jnp.stack(pieces).reshape(3, 3, CH, CH)
    grad_bias = jnp.sum(grad_out.astype(jnp.float32), axis=0)
    return (output, grad_weight, grad_bias)
```

```python
import functools

import jax
import jax.numpy as jnp
from jax import lax
from jax.experimental import pallas as pl
from jax.experimental.pallas import tpu as pltpu
from jax.sharding import PartitionSpec as P

MESH = pl.DeviceIdType.MESH
NT = (((1,), (1,)), ((), ()))


def shift_cols(value, by):
    cols = value.shape[1]
    col = lax.broadcasted_iota(jnp.int32, value.shape, 1)
    if by < 0:
        return jnp.where(col == 0, 0.0, pltpu.roll(value, 1, 1))
    return jnp.where(col == cols - 1, 0.0, pltpu.roll(value, cols - 1, 1))


def lanes(q, cols, count=1):
    return pl.ds(pl.multiple_of(q * cols, cols), count * cols)


def store_shifts(grads, place, grad):
    wide = grad.astype(jnp.float32)
    grads[0, :, place] = shift_cols(wide, 1).astype(jnp.bfloat16)
    grads[2, :, place] = shift_cols(wide, -1).astype(jnp.bfloat16)


def rows_tap(rows, grads, a, b, start, count):
    cols, depth = rows.shape[1], rows.shape[2]
    window = rows[pl.ds(start + a, count)].reshape(count * cols, depth)
    return jnp.dot(
        grads[b, :, lanes(start, cols, count)], window, preferred_element_type=jnp.float32
    )


def late_row(block, n_f):
    return block * n_f + jnp.where(block > 0, 0, n_f - 1)


def early_row(block, n_f):
    return block * n_f + jnp.where(block > 0, 1, 0)


def gather_kernel(
    n_f, n_s,
    image, weight, bias_in, cotangent,
    rows, grads, gw_own, out,
    w, bias, cot, part, peer, act,
    load_sem, ready_z, ready_x, row_send, row_recv, x_send, sum_send, sum_recv,
    g_send, g_recv, h_send, h_recv, out_send, out_recv,
):
    p, s, c = lax.axis_index("filt"), lax.axis_index("sp"), lax.axis_index("in")
    sibling = 1 - c
    cols, depth = rows.shape[1], rows.shape[2]
    o = w.shape[2]
    half_c = out.shape[1]
    total = n_f * n_s
    first = s * n_f
    last = n_f - 1
    x_peers = [lax.rem(s + d, n_s) for d in range(1, n_s)]

    load_row = pltpu.make_async_copy(image.at[0], rows.at[1 + first + p], load_sem.at[0])
    load_w = pltpu.make_async_copy(
        weight.at[:, :, :, pl.ds(pl.multiple_of(c * depth, depth), depth)], w, load_sem.at[1]
    )
    load_cot = pltpu.make_async_copy(cotangent, cot, load_sem.at[2])
    load_bias = pltpu.make_async_copy(bias_in, bias, load_sem.at[3])
    load_row.start()
    load_w.start()
    load_cot.start()
    load_bias.start()

    barrier = pltpu.get_barrier_semaphore()

    @pl.when(p < last)
    def _():
        pl.semaphore_signal(barrier, 1, device_id={"filt": p + 1}, device_id_type=MESH)

    for peer_s in x_peers:
        @pl.when(peer_s > s)
        def _():
            pl.semaphore_signal(barrier, 1, device_id={"sp": peer_s}, device_id_type=MESH)

    pl.semaphore_signal(barrier, 1, device_id={"in": sibling}, device_id_type=MESH)
    pl.semaphore_wait(barrier, 1 + s + jnp.where(p > 0, 1, 0))

    piece = cols // 2

    def row_copy(q, h, way, where, send):
        slot = rows.at[1 + q, pl.ds(h * piece, piece)]
        return pltpu.make_async_remote_copy(
            src_ref=slot, dst_ref=slot, send_sem=send, recv_sem=row_recv.at[q, h],
            device_id={way: where}, device_id_type=MESH,
        )

    def to_right(q, h):
        return row_copy(q, h, "filt", p + 1, row_send.at[0, q, h])

    def to_left(q, h):
        return row_copy(q, h, "filt", p - 1, row_send.at[1, q, h])

    def to_x(q, h, d):
        return row_copy(first + q, h, "sp", x_peers[d], x_send.at[d, q, h])

    def wait_row(q, h):
        row_copy(q, h, "filt", p, row_send.at[0, 0, 0]).wait_recv()

    def crosses(q):
        return ((q > 0) & (q < last)) | (q == p)

    def pass_on(q, h, right, left):
        if right:
            @pl.when(p < last)
            def _():
                to_right(first + q, h).start()
        if left:
            @pl.when(p > 0)
            def _():
                to_left(first + q, h).start()

        @pl.when(crosses(q))
        def _():
            for d in range(n_s - 1):
                to_x(q, h, d).start()

    def own_copy(h, way, where, send):
        place = pl.ds(h * piece, piece)
        return pltpu.make_async_remote_copy(
            src_ref=image.at[0, place], dst_ref=rows.at[1 + first + p, place],
            send_sem=send, recv_sem=row_recv.at[first + p, h],
            device_id={way: where}, device_id_type=MESH,
        )

    def own_to_x(up):
        for d in range(n_s - 1):
            @pl.when((x_peers[d] > s) if up else (x_peers[d] < s))
            def _():
                for h in range(2):
                    own_copy(h, "sp", x_peers[d], x_send.at[d, p, h]).start()

    @pl.when(p > 0)
    def _():
        for h in range(2):
            own_copy(h, "filt", p - 1, row_send.at[1, first + p, h]).start()
        pl.semaphore_signal(ready_z, 1, device_id={"filt": p - 1}, device_id_type=MESH)

    own_to_x(False)
    for peer_s in x_peers:
        @pl.when(peer_s < s)
        def _():
            pl.semaphore_signal(ready_x, 1, device_id={"sp": peer_s}, device_id_type=MESH)

    @pl.when(p < last)
    def _():
        pl.semaphore_wait(ready_z, 1)
        for h in range(2):
            own_copy(h, "filt", p + 1, row_send.at[0, first + p, h]).start()

    @pl.when(s < n_s - 1)
    def _():
        pl.semaphore_wait(ready_x, n_s - 1 - s)

    own_to_x(True)
    load_row.wait()

    zero = jnp.zeros((cols, depth), rows.dtype)
    rows[0] = zero
    rows[total + 1] = zero

    @pl.loop(0, n_f + 2)
    def _(r):
        part[r] = jnp.zeros((o, cols), jnp.float32)

    load_w.wait()

    def add_tap(q, a, r):
        sums = lax.dot_general(
            w[a].reshape(3 * o, depth), rows[1 + q], NT, preferred_element_type=jnp.float32
        )
        part[r + 1] += shift_cols(sums[:o], -1) + sums[o:2 * o] + shift_cols(sums[2 * o:], 1)

    def add_row(q):
        for a in range(3):
            add_tap(first + q, a, q - a + 1)

    def sum_copy(r):
        return pltpu.make_async_remote_copy(
            src_ref=part.at[r + 1], dst_ref=peer.at[r], send_sem=sum_send.at[r], recv_sem=sum_recv.at[r],
            device_id={"in": sibling}, device_id_type=MESH,
        )

    def out_copy(r):
        return pltpu.make_async_remote_copy(
            src_ref=act.at[r, :, pl.ds(pl.multiple_of(c * half_c, half_c), half_c)],
            dst_ref=out.at[pl.ds(pl.multiple_of(p * o, o), o), :],
            send_sem=out_send.at[r], recv_sem=out_recv.at[p],
            device_id={"filt": r}, device_id_type=MESH,
        )

    own_out = pltpu.make_async_copy(
        act.at[p, :, pl.ds(pl.multiple_of(c * half_c, half_c), half_c)],
        out.at[pl.ds(pl.multiple_of(p * o, o), o), :],
        load_sem.at[0],
    )

    half_o = o // 2

    def g_half(q, core):
        return grads.at[1, pl.ds(pl.multiple_of(core * half_o, half_o), half_o), lanes(q, cols)]

    def g_copy(q, d):
        place = g_half(q, c)
        return pltpu.make_async_remote_copy(
            src_ref=place, dst_ref=place, send_sem=g_send.at[d, q], recv_sem=g_recv.at[q],
            device_id={"sp": x_peers[d]}, device_id_type=MESH,
        )

    def h_copy(q, core):
        place = g_half(q, core)
        return pltpu.make_async_remote_copy(
            src_ref=place, dst_ref=place, send_sem=h_send.at[q], recv_sem=h_recv.at[q],
            device_id={"in": sibling}, device_id_type=MESH,
        )

    def done_at(r):
        low = jnp.where(s == 0, jnp.maximum(p, 1), jnp.maximum(p, n_f - p))
        high = jnp.where(
            s == n_s - 1, jnp.maximum(last - p, 1), jnp.maximum(last - p, p + 1)
        )
        return jnp.where(r == 0, low, jnp.where(r == last, high, jnp.abs(r - p) + 1))

    def finish(r):
        sum_copy(r).wait_recv()
        bias_all = jnp.broadcast_to(bias[...], (cols, o)).T
        shifted = part[r + 1] + peer[r] + bias_all
        sig = jax.nn.sigmoid(shifted)
        slope = sig * (1.0 + shifted * (1.0 - sig))
        grad = (cot[r].astype(jnp.float32) * slope).astype(jnp.bfloat16)
        place = lanes(first + r, cols)
        grads[1, :, place] = grad
        act[r] = (shifted * sig).astype(jnp.bfloat16)
        for d in range(n_s - 1):
            g_copy(first + r, d).start()

        store_shifts(grads, place, grad)

    def send_out(r):
        @pl.when(r == p)
        def _():
            own_out.start()

        @pl.when(r != p)
        def _():
            out_copy(r).start()

    add_row(p)
    load_cot.wait()
    load_bias.wait()

    def relay(t):
        @pl.when(t == p + 1)
        def _():
            for block in x_peers:
                for h in range(2):
                    wait_row(block * n_f, h)

                    @pl.when(p < last)
                    def _():
                        to_right(block * n_f, h).start()

        @pl.when(t == n_f - p)
        def _():
            for block in x_peers:
                for h in range(2):
                    wait_row(block * n_f + last, h)

                    @pl.when(p > 0)
                    def _():
                        to_left(block * n_f + last, h).start()

    def add_edges(t):
        @pl.when((t == p + 1) & (s < n_s - 1))
        def _():
            add_tap(first + n_f, 2, last)

        @pl.when((t == n_f - p) & (s > 0))
        def _():
            add_tap(first - 1, 0, 0)

    def start_sums(t):
        @pl.loop(0, n_f)
        def _(r):
            @pl.when(done_at(r) == t)
            def _():
                sum_copy(r).start()

    def finish_rows(t):
        @pl.loop(0, n_f)
        def _(r):
            @pl.when(done_at(r) == t)
            def _():
                finish(r)

    @pl.loop(1, n_f)
    def _(t):
        for h in range(2):
            @pl.when(p - t >= 0)
            def _():
                wait_row(first + p - t, h)
                pass_on(p - t, h, True, False)

            @pl.when(p + t < n_f)
            def _():
                wait_row(first + p + t, h)
                pass_on(p + t, h, False, True)

        relay(t)

        @pl.when(p - t >= 0)
        def _():
            add_row(p - t)

        @pl.when(p + t < n_f)
        def _():
            add_row(p + t)

        add_edges(t)
        start_sums(t)
        finish_rows(t - 1)

    def own_rows():
        @pl.loop(0, 9)
        def _(k):
            gw_own[k] = rows_tap(rows, grads, k // 3, lax.rem(k, 3), early_row(s, n_f), n_f - 1)

    finish_rows(n_f - 1)
    if n_s <= 2:
        own_rows()
    relay(n_f)
    add_edges(n_f)
    start_sums(n_f)

    @pl.loop(0, n_f)
    def _(r):
        @pl.when(done_at(r) < n_f)
        def _():
            send_out(r)

    finish_rows(n_f)

    @pl.loop(0, n_f)
    def _(r):
        @pl.when(done_at(r) == n_f)
        def _():
            send_out(r)

    if n_s > 2:
        own_rows()

    def share_grad(q):
        g_copy(q, 0).wait_recv()
        h_copy(q, c).start()

    def take_grad(q):
        h_copy(q, sibling).wait_recv()
        place = lanes(q, cols)
        store_shifts(grads, place, grads[1, :, place])

    for block in x_peers:
        start = early_row(block, n_f)

        @pl.loop(1, last)
        def _(q):
            for h in range(2):
                wait_row(block * n_f + q, h)

        @pl.loop(0, n_f - 1)
        def _(q):
            share_grad(start + q)

        @pl.loop(0, n_f - 1)
        def _(q):
            take_grad(start + q)

        @pl.loop(0, 9)
        def _(k):
            gw_own[k] += rows_tap(rows, grads, k // 3, lax.rem(k, 3), start, n_f - 1)

    for block in x_peers:
        share_grad(late_row(block, n_f))
        take_grad(late_row(block, n_f))

    @pl.loop(0, n_f)
    def _(r):
        sum_copy(r).wait_send()

        @pl.when(r == p)
        def _():
            own_out.wait()

        @pl.when(r != p)
        def _():
            out_copy(r).wait_send()
            pltpu.make_async_remote_copy(
                src_ref=act.at[r, :, pl.ds(0, half_c)],
                dst_ref=out.at[pl.ds(pl.multiple_of(r * o, o), o), :],
                send_sem=out_send.at[r], recv_sem=out_recv.at[r],
                device_id={"filt": r}, device_id_type=MESH,
            ).wait_recv()

        for d in range(n_s - 1):
            g_copy(first + r, d).wait_send()

            @pl.when(crosses(r))
            def _():
                for h in range(2):
                    to_x(r, h, d).wait_send()

        @pl.when((r <= p) & (p < last))
        def _():
            for h in range(2):
                to_right(first + r, h).wait_send()

        @pl.when((r >= p) & (p > 0))
        def _():
            for h in range(2):
                to_left(first + r, h).wait_send()

    for block in x_peers:
        @pl.loop(0, n_f)
        def _(q):
            h_copy(block * n_f + q, c).wait_send()

        for h in range(2):
            @pl.when(p < last)
            def _():
                to_right(block * n_f, h).wait_send()

            @pl.when(p > 0)
            def _():
                to_left(block * n_f + last, h).wait_send()


def finish_kernel(n_f, n_s, rows, grads, gw_own, out_in, gw, gb, out, total, sem, out_sem):
    out_copy = pltpu.make_async_copy(out_in, out.at[0], out_sem)
    out_copy.start()

    late = [(n_f - 1, min(n_s, 2))] + [(block * n_f, 1) for block in range(2, n_s)]

    def gw_copy(k):
        return pltpu.make_async_copy(total.at[k], gw.at[k // 3, lax.rem(k, 3)], sem.at[k])

    @pl.loop(0, 9)
    def _(k):
        value = gw_own[k]
        for start, count in late:
            value = value + rows_tap(rows, grads, k // 3, lax.rem(k, 3), start, count)
        total[k] = value
        gw_copy(k).start()

    gb[...] = lax.dot_general(
        jnp.ones((8, grads.shape[2]), jnp.bfloat16), grads[1], NT, preferred_element_type=jnp.float32
    )[:1]

    @pl.loop(0, 9)
    def _(k):
        gw_copy(k).wait()

    out_copy.wait()


def on_device(image, weight, bias, cotangent):
    n_f, n_s, n_in = (lax.axis_size(name) for name in ("filt", "sp", "in"))
    row_count, o, cols = cotangent.shape
    depth = image.shape[2]
    total = n_f * n_s
    any_space = pl.BlockSpec(memory_space=pl.ANY)
    vmem = pl.BlockSpec(memory_space=pltpu.VMEM)
    hbm = pl.BlockSpec(memory_space=pltpu.HBM)
    dma = pltpu.SemaphoreType.DMA
    between = pl.pallas_call(
        functools.partial(gather_kernel, n_f, n_s),
        out_shape=(
            pltpu.VMEM((total + 2, cols, depth), jnp.bfloat16),
            pltpu.VMEM((3, o, total * cols), jnp.bfloat16),
            pltpu.VMEM((9, o, depth), jnp.float32),
            pltpu.VMEM((n_f * o, cols // n_in), jnp.bfloat16),
        ),
        in_specs=[hbm, hbm, hbm, hbm],
        out_specs=(vmem,) * 4,
        scratch_shapes=[
            pltpu.VMEM((3, 3, o, depth), jnp.bfloat16),
            pltpu.VMEM((1, o), jnp.float32),
            pltpu.VMEM((n_f, o, cols), jnp.bfloat16),
            pltpu.VMEM((n_f + 2, o, cols), jnp.float32),
            pltpu.VMEM((n_f, o, cols), jnp.float32),
            pltpu.VMEM((n_f, o, cols), jnp.bfloat16),
            dma((4,)),
            pltpu.SemaphoreType.REGULAR,
            pltpu.SemaphoreType.REGULAR,
            dma((2, total, 2)),
            dma((total, 2)),
            dma((n_s - 1, n_f, 2)),
            dma((n_f,)),
            dma((n_f,)),
            dma((n_s - 1, total)),
            dma((total,)),
            dma((total,)),
            dma((total,)),
            dma((n_f,)),
            dma((n_f,)),
        ],
        compiler_params=pltpu.CompilerParams(
            collective_id=0, has_side_effects=True, vmem_limit_bytes=24 * 1024 * 1024
        ),
        name="gather",
    )(*(
        pltpu.with_memory_space_constraint(x, pltpu.HBM)
        for x in (image, weight, bias.reshape(1, o), cotangent)
    ))
    grad_weight, grad_bias, output = pl.pallas_call(
        functools.partial(finish_kernel, n_f, n_s),
        out_shape=(
            jax.ShapeDtypeStruct((3, 3, o, depth), jnp.float32),
            jax.ShapeDtypeStruct((1, o), jnp.float32),
            jax.ShapeDtypeStruct((1, n_f * o, cols // n_in), jnp.bfloat16),
        ),
        in_specs=[vmem] * 4,
        out_specs=(any_space, vmem, any_space),
        scratch_shapes=[
            pltpu.VMEM((9, o, depth), jnp.float32),
            dma((9,)),
            dma(()),
        ],
        compiler_params=pltpu.CompilerParams(vmem_limit_bytes=20 * 1024 * 1024),
        name="finish",
    )(*between)
    return (output, grad_weight, grad_bias.reshape(o))


def solution(mesh):
    placed = (
        P(("groups", "sp", "filt"), None, "in"),
        P(None, None, "filt", None),
        P("filt"),
        P(("groups", "sp"), "filt", None),
    )
    return jax.shard_map(
        on_device,
        mesh=mesh,
        in_specs=placed,
        out_specs=(
            P(("groups", "sp", "filt"), None, "in"),
            P("groups", None, "filt", "in"),
            P(("groups", "filt")),
        ),
        check_vma=False,
    )
```

```python
import functools

import jax
import jax.numpy as jnp
from jax import lax
from jax.experimental import pallas as pl
from jax.experimental.pallas import tpu as pltpu
from jax.sharding import PartitionSpec as P

MESH = pl.DeviceIdType.MESH
NT = (((1,), (1,)), ((), ()))


def shift_cols(value, by):
    cols = value.shape[1]
    col = lax.broadcasted_iota(jnp.int32, value.shape, 1)
    if by < 0:
        return jnp.where(col == 0, 0.0, pltpu.roll(value, 1, 1))
    return jnp.where(col == cols - 1, 0.0, pltpu.roll(value, cols - 1, 1))


def lanes(q, cols, count=1):
    return pl.ds(pl.multiple_of(q * cols, cols), count * cols)


def store_shifts(grads, place, grad):
    wide = grad.astype(jnp.float32)
    grads[0, :, place] = shift_cols(wide, 1).astype(jnp.bfloat16)
    grads[2, :, place] = shift_cols(wide, -1).astype(jnp.bfloat16)


def rows_tap(rows, grads, a, start, count):
    cols, depth = rows.shape[1], rows.shape[2]
    o = grads.shape[1]
    window = rows[pl.ds(start + a, count)].reshape(count * cols, depth)
    left = grads[:, :, lanes(start, cols, count)].reshape(3 * o, count * cols)
    return jnp.dot(left, window, preferred_element_type=jnp.float32).reshape(3, o, depth)


def bias_tap(grads, cols, start, count):
    ones = jnp.ones((8, count * cols), jnp.bfloat16)
    return lax.dot_general(
        ones, grads[1, :, lanes(start, cols, count)], NT, preferred_element_type=jnp.float32
    )


def late_row(block, n_f):
    return block * n_f + jnp.where(block > 0, 0, n_f - 1)


def early_row(block, n_f):
    return block * n_f + jnp.where(block > 0, 1, 0)


def gather_kernel(
    n_f, n_s,
    image, weight, bias_in, cotangent,
    rows, grads, gw_own, gb_own, out,
    w, bias, cot, part, peer, act,
    load_sem, ready_z, ready_x, row_send, row_recv, x_send, sum_send, sum_recv,
    g_send, g_recv, h_send, h_recv, out_send, out_recv,
):
    p, s, c = lax.axis_index("filt"), lax.axis_index("sp"), lax.axis_index("in")
    sibling = 1 - c
    cols, depth = rows.shape[1], rows.shape[2]
    o = w.shape[2]
    half_c = out.shape[1]
    total = n_f * n_s
    first = s * n_f
    last = n_f - 1
    x_peers = [lax.rem(s + d, n_s) for d in range(1, n_s)]

    load_row = pltpu.make_async_copy(image.at[0], rows.at[1 + first + p], load_sem.at[0])
    load_w = pltpu.make_async_copy(
        weight.at[:, :, :, pl.ds(pl.multiple_of(c * depth, depth), depth)], w, load_sem.at[1]
    )
    load_cot = pltpu.make_async_copy(cotangent, cot, load_sem.at[2])
    load_bias = pltpu.make_async_copy(bias_in, bias, load_sem.at[3])
    load_row.start()
    load_w.start()
    load_cot.start()
    load_bias.start()

    barrier = pltpu.get_barrier_semaphore()

    @pl.when(p < last)
    def _():
        pl.semaphore_signal(barrier, 1, device_id={"filt": p + 1}, device_id_type=MESH)

    for peer_s in x_peers:
        @pl.when(peer_s > s)
        def _():
            pl.semaphore_signal(barrier, 1, device_id={"sp": peer_s}, device_id_type=MESH)

    pl.semaphore_signal(barrier, 1, device_id={"in": sibling}, device_id_type=MESH)
    pl.semaphore_wait(barrier, 1 + s + jnp.where(p > 0, 1, 0))

    piece = cols // 2

    def row_copy(q, h, way, where, send):
        slot = rows.at[1 + q, pl.ds(h * piece, piece)]
        return pltpu.make_async_remote_copy(
            src_ref=slot, dst_ref=slot, send_sem=send, recv_sem=row_recv.at[q, h],
            device_id={way: where}, device_id_type=MESH,
        )

    def to_right(q, h):
        return row_copy(q, h, "filt", p + 1, row_send.at[0, q, h])

    def to_left(q, h):
        return row_copy(q, h, "filt", p - 1, row_send.at[1, q, h])

    def to_x(q, h, d):
        return row_copy(first + q, h, "sp", x_peers[d], x_send.at[d, q, h])

    def wait_row(q, h):
        row_copy(q, h, "filt", p, row_send.at[0, 0, 0]).wait_recv()

    def crosses(q, h):
        return ((q > 0) & (q < last)) | (q == p) | (h == 0)

    def pass_on(q, h, right, left):
        if right:
            @pl.when(p < last)
            def _():
                to_right(first + q, h).start()
        if left:
            @pl.when(p > 0)
            def _():
                to_left(first + q, h).start()

        @pl.when(crosses(q, h))
        def _():
            for d in range(n_s - 1):
                to_x(q, h, d).start()

    def own_copy(h, way, where, send):
        place = pl.ds(h * piece, piece)
        return pltpu.make_async_remote_copy(
            src_ref=image.at[0, place], dst_ref=rows.at[1 + first + p, place],
            send_sem=send, recv_sem=row_recv.at[first + p, h],
            device_id={way: where}, device_id_type=MESH,
        )

    def own_to_x(up):
        for d in range(n_s - 1):
            @pl.when((x_peers[d] > s) if up else (x_peers[d] < s))
            def _():
                for h in range(2):
                    own_copy(h, "sp", x_peers[d], x_send.at[d, p, h]).start()

    @pl.when(p > 0)
    def _():
        for h in range(2):
            own_copy(h, "filt", p - 1, row_send.at[1, first + p, h]).start()
        pl.semaphore_signal(ready_z, 1, device_id={"filt": p - 1}, device_id_type=MESH)

    own_to_x(False)
    for peer_s in x_peers:
        @pl.when(peer_s < s)
        def _():
            pl.semaphore_signal(ready_x, 1, device_id={"sp": peer_s}, device_id_type=MESH)

    @pl.when(p < last)
    def _():
        pl.semaphore_wait(ready_z, 1)
        for h in range(2):
            own_copy(h, "filt", p + 1, row_send.at[0, first + p, h]).start()

    @pl.when(s < n_s - 1)
    def _():
        pl.semaphore_wait(ready_x, n_s - 1 - s)

    own_to_x(True)
    load_row.wait()

    zero = jnp.zeros((cols, depth), rows.dtype)
    rows[0] = zero
    rows[total + 1] = zero

    @pl.loop(0, n_f + 2)
    def _(r):
        part[r] = jnp.zeros((o, cols), jnp.float32)

    load_w.wait()

    def add_tap(q, a, r):
        sums = lax.dot_general(
            w[a].reshape(3 * o, depth), rows[1 + q], NT, preferred_element_type=jnp.float32
        )
        part[r + 1] += shift_cols(sums[:o], -1) + sums[o:2 * o] + shift_cols(sums[2 * o:], 1)

    def add_row(q):
        sums = lax.dot_general(
            w[...].reshape(9 * o, depth), rows[1 + first + q], NT, preferred_element_type=jnp.float32
        )
        for a in range(3):
            left, middle, right = (sums[(3 * a + b) * o:(3 * a + b + 1) * o] for b in range(3))
            part[q - a + 2] += shift_cols(left, -1) + middle + shift_cols(right, 1)

    def sum_copy(r):
        return pltpu.make_async_remote_copy(
            src_ref=part.at[r + 1], dst_ref=peer.at[r], send_sem=sum_send.at[r], recv_sem=sum_recv.at[r],
            device_id={"in": sibling}, device_id_type=MESH,
        )

    def out_copy(r):
        return pltpu.make_async_remote_copy(
            src_ref=act.at[r, :, pl.ds(pl.multiple_of(c * half_c, half_c), half_c)],
            dst_ref=out.at[pl.ds(pl.multiple_of(p * o, o), o), :],
            send_sem=out_send.at[r], recv_sem=out_recv.at[p],
            device_id={"filt": r}, device_id_type=MESH,
        )

    own_out = pltpu.make_async_copy(
        act.at[p, :, pl.ds(pl.multiple_of(c * half_c, half_c), half_c)],
        out.at[pl.ds(pl.multiple_of(p * o, o), o), :],
        load_sem.at[0],
    )

    half_o = o // 2

    def g_half(q, core):
        return grads.at[1, pl.ds(pl.multiple_of(core * half_o, half_o), half_o), lanes(q, cols)]

    def g_copy(q, d):
        place = g_half(q, c)
        return pltpu.make_async_remote_copy(
            src_ref=place, dst_ref=place, send_sem=g_send.at[d, q], recv_sem=g_recv.at[q],
            device_id={"sp": x_peers[d]}, device_id_type=MESH,
        )

    def h_copy(q, core):
        place = g_half(q, core)
        return pltpu.make_async_remote_copy(
            src_ref=place, dst_ref=place, send_sem=h_send.at[q], recv_sem=h_recv.at[q],
            device_id={"in": sibling}, device_id_type=MESH,
        )

    def done_at(r):
        low = jnp.where(s == 0, jnp.maximum(p, 1), jnp.maximum(p, n_f - p))
        high = jnp.where(
            s == n_s - 1, jnp.maximum(last - p, 1), jnp.maximum(last - p, p + 1)
        )
        return jnp.where(r == 0, low, jnp.where(r == last, high, jnp.abs(r - p) + 1))

    def finish(r):
        sum_copy(r).wait_recv()
        bias_all = jnp.broadcast_to(bias[...], (cols, o)).T
        shifted = part[r + 1] + peer[r] + bias_all
        sig = jax.nn.sigmoid(shifted)
        slope = sig * (1.0 + shifted * (1.0 - sig))
        grad = (cot[r].astype(jnp.float32) * slope).astype(jnp.bfloat16)
        place = lanes(first + r, cols)
        grads[1, :, place] = grad
        act[r] = (shifted * sig).astype(jnp.bfloat16)
        for d in range(n_s - 1):
            g_copy(first + r, d).start()

        store_shifts(grads, place, grad)

    def send_out(r):
        @pl.when(r == p)
        def _():
            own_out.start()

        @pl.when(r != p)
        def _():
            out_copy(r).start()

    add_row(p)
    load_cot.wait()
    load_bias.wait()

    def relay(t):
        @pl.when(t == p + 1)
        def _():
            for block in x_peers:
                wait_row(block * n_f, 1)

                @pl.when(p < last)
                def _():
                    to_right(block * n_f, 1).start()

                wait_row(block * n_f, 0)

        @pl.when(t == n_f - p)
        def _():
            for block in x_peers:
                wait_row(block * n_f + last, 1)

                @pl.when(p > 0)
                def _():
                    to_left(block * n_f + last, 1).start()

                wait_row(block * n_f + last, 0)

    def add_edges(t):
        @pl.when((t == p + 1) & (s < n_s - 1))
        def _():
            add_tap(first + n_f, 2, last)

        @pl.when((t == n_f - p) & (s > 0))
        def _():
            add_tap(first - 1, 0, 0)

    def start_sums(t):
        @pl.loop(0, n_f)
        def _(r):
            @pl.when(done_at(r) == t)
            def _():
                sum_copy(r).start()

    def finish_rows(t):
        @pl.loop(0, n_f)
        def _(r):
            @pl.when(done_at(r) == t)
            def _():
                finish(r)

    @pl.loop(1, n_f)
    def _(t):
        for h in range(2):
            @pl.when(p - t >= 0)
            def _():
                wait_row(first + p - t, h)
                pass_on(p - t, h, True, False)

            @pl.when(p + t < n_f)
            def _():
                wait_row(first + p + t, h)
                pass_on(p + t, h, False, True)

        relay(t)

        @pl.when(p - t >= 0)
        def _():
            add_row(p - t)

        @pl.when(p + t < n_f)
        def _():
            add_row(p + t)

        add_edges(t)
        start_sums(t)
        finish_rows(t - 1)

    early = early_row(s, n_f)

    def own_rows(a):
        gw_own[3 * a:3 * a + 3] = rows_tap(rows, grads, a, early, n_f - 1)

    def send_outs(when):
        @pl.loop(0, n_f)
        def _(r):
            @pl.when(when(done_at(r)))
            def _():
                send_out(r)

    finish_rows(n_f - 1)
    send_outs(lambda done: done < n_f)
    relay(n_f)
    add_edges(n_f)
    start_sums(n_f)
    covering = 2 if n_s <= 2 else 0
    for a in range(covering):
        own_rows(a)
    finish_rows(n_f)
    send_outs(lambda done: done == n_f)
    for a in range(covering, 3):
        own_rows(a)
    gb_own[...] = bias_tap(grads, cols, early, n_f - 1)

    def share_grad(q):
        g_copy(q, 0).wait_recv()
        h_copy(q, c).start()

    def take_grad(q):
        h_copy(q, sibling).wait_recv()
        place = lanes(q, cols)
        store_shifts(grads, place, grads[1, :, place])

    for block in x_peers:
        start = early_row(block, n_f)

        @pl.loop(1, last)
        def _(q):
            for h in range(2):
                wait_row(block * n_f + q, h)

        @pl.loop(0, n_f - 1)
        def _(q):
            share_grad(start + q)

        @pl.loop(0, n_f - 1)
        def _(q):
            take_grad(start + q)

        for a in range(3):
            gw_own[3 * a:3 * a + 3] += rows_tap(rows, grads, a, start, n_f - 1)

        gb_own[...] += bias_tap(grads, cols, start, n_f - 1)

    for block in x_peers:
        share_grad(late_row(block, n_f))
        take_grad(late_row(block, n_f))

    @pl.loop(0, n_f)
    def _(r):
        sum_copy(r).wait_send()

        @pl.when(r == p)
        def _():
            own_out.wait()

        @pl.when(r != p)
        def _():
            out_copy(r).wait_send()
            pltpu.make_async_remote_copy(
                src_ref=act.at[r, :, pl.ds(0, half_c)],
                dst_ref=out.at[pl.ds(pl.multiple_of(r * o, o), o), :],
                send_sem=out_send.at[r], recv_sem=out_recv.at[r],
                device_id={"filt": r}, device_id_type=MESH,
            ).wait_recv()

        for d in range(n_s - 1):
            g_copy(first + r, d).wait_send()

            for h in range(2):
                @pl.when(crosses(r, h))
                def _():
                    to_x(r, h, d).wait_send()

        @pl.when((r <= p) & (p < last))
        def _():
            for h in range(2):
                to_right(first + r, h).wait_send()

        @pl.when((r >= p) & (p > 0))
        def _():
            for h in range(2):
                to_left(first + r, h).wait_send()

    for block in x_peers:
        @pl.loop(0, n_f)
        def _(q):
            h_copy(block * n_f + q, c).wait_send()

        @pl.when(p < last)
        def _():
            to_right(block * n_f, 1).wait_send()

        @pl.when(p > 0)
        def _():
            to_left(block * n_f + last, 1).wait_send()


def finish_kernel(n_f, n_s, rows, grads, gw_own, gb_own, out_in, gw, gb, out, total, sem, out_sem):
    cols = rows.shape[1]
    out_copy = pltpu.make_async_copy(out_in, out.at[0], out_sem)
    out_copy.start()

    late = [(n_f - 1, min(n_s, 2))] + [(block * n_f, 1) for block in range(2, n_s)]

    def gw_copy(a):
        return pltpu.make_async_copy(total.at[a], gw.at[a], sem.at[a])

    for a in range(3):
        value = gw_own[3 * a:3 * a + 3]
        for start, count in late:
            value = value + rows_tap(rows, grads, a, start, count)
        total[a] = value
        gw_copy(a).start()

    bias = gb_own[...]
    for start, count in late:
        bias = bias + bias_tap(grads, cols, start, count)
    gb[...] = bias[:1]

    for a in range(3):
        gw_copy(a).wait()

    out_copy.wait()


def on_device(image, weight, bias, cotangent):
    n_f, n_s, n_in = (lax.axis_size(name) for name in ("filt", "sp", "in"))
    row_count, o, cols = cotangent.shape
    depth = image.shape[2]
    total = n_f * n_s
    any_space = pl.BlockSpec(memory_space=pl.ANY)
    vmem = pl.BlockSpec(memory_space=pltpu.VMEM)
    hbm = pl.BlockSpec(memory_space=pltpu.HBM)
    dma = pltpu.SemaphoreType.DMA
    between = pl.pallas_call(
        functools.partial(gather_kernel, n_f, n_s),
        out_shape=(
            pltpu.VMEM((total + 2, cols, depth), jnp.bfloat16),
            pltpu.VMEM((3, o, total * cols), jnp.bfloat16),
            pltpu.VMEM((9, o, depth), jnp.float32),
            pltpu.VMEM((8, o), jnp.float32),
            pltpu.VMEM((n_f * o, cols // n_in), jnp.bfloat16),
        ),
        in_specs=[hbm, hbm, hbm, hbm],
        out_specs=(vmem,) * 5,
        scratch_shapes=[
            pltpu.VMEM((3, 3, o, depth), jnp.bfloat16),
            pltpu.VMEM((1, o), jnp.float32),
            pltpu.VMEM((n_f, o, cols), jnp.bfloat16),
            pltpu.VMEM((n_f + 2, o, cols), jnp.float32),
            pltpu.VMEM((n_f, o, cols), jnp.float32),
            pltpu.VMEM((n_f, o, cols), jnp.bfloat16),
            dma((4,)),
            pltpu.SemaphoreType.REGULAR,
            pltpu.SemaphoreType.REGULAR,
            dma((2, total, 2)),
            dma((total, 2)),
            dma((n_s - 1, n_f, 2)),
            dma((n_f,)),
            dma((n_f,)),
            dma((n_s - 1, total)),
            dma((total,)),
            dma((total,)),
            dma((total,)),
            dma((n_f,)),
            dma((n_f,)),
        ],
        compiler_params=pltpu.CompilerParams(
            collective_id=0, has_side_effects=True, vmem_limit_bytes=24 * 1024 * 1024
        ),
        name="gather",
    )(*(
        pltpu.with_memory_space_constraint(x, pltpu.HBM)
        for x in (image, weight, bias.reshape(1, o), cotangent)
    ))
    grad_weight, grad_bias, output = pl.pallas_call(
        functools.partial(finish_kernel, n_f, n_s),
        out_shape=(
            jax.ShapeDtypeStruct((3, 3, o, depth), jnp.float32),
            jax.ShapeDtypeStruct((1, o), jnp.float32),
            jax.ShapeDtypeStruct((1, n_f * o, cols // n_in), jnp.bfloat16),
        ),
        in_specs=[vmem] * 5,
        out_specs=(any_space, vmem, any_space),
        scratch_shapes=[
            pltpu.VMEM((3, 3, o, depth), jnp.float32),
            dma((3,)),
            dma(()),
        ],
        compiler_params=pltpu.CompilerParams(vmem_limit_bytes=20 * 1024 * 1024),
        name="finish",
    )(*between)
    return (output, grad_weight, grad_bias.reshape(o))


def solution(mesh):
    placed = (
        P(("groups", "sp", "filt"), None, "in"),
        P(None, None, "filt", None),
        P("filt"),
        P(("groups", "sp"), "filt", None),
    )
    return jax.shard_map(
        on_device,
        mesh=mesh,
        in_specs=placed,
        out_specs=(
            P(("groups", "sp", "filt"), None, "in"),
            P("groups", None, "filt", "in"),
            P(("groups", "filt")),
        ),
        check_vma=False,
    )
```

```python
import functools

import jax
import jax.numpy as jnp
from jax import lax
from jax.experimental import pallas as pl
from jax.experimental.pallas import tpu as pltpu
from jax.sharding import PartitionSpec as P

MESH = pl.DeviceIdType.MESH
NT = (((1,), (1,)), ((), ()))


def shift_cols(value, by):
    cols = value.shape[1]
    col = lax.broadcasted_iota(jnp.int32, value.shape, 1)
    if by < 0:
        return jnp.where(col == 0, 0.0, pltpu.roll(value, 1, 1))
    return jnp.where(col == cols - 1, 0.0, pltpu.roll(value, cols - 1, 1))


def lanes(q, cols, count=1):
    return pl.ds(pl.multiple_of(q * cols, cols), count * cols)


def store_shifts(grads, place, grad):
    wide = grad.astype(jnp.float32)
    grads[0, :, place] = shift_cols(wide, 1).astype(jnp.bfloat16)
    grads[2, :, place] = shift_cols(wide, -1).astype(jnp.bfloat16)


def rows_tap(rows, grads, a, start, count):
    cols, depth = rows.shape[1], rows.shape[2]
    o = grads.shape[1]
    window = rows[pl.ds(start + a, count)].reshape(count * cols, depth)
    left = grads[:, :, lanes(start, cols, count)].reshape(3 * o, count * cols)
    return jnp.dot(left, window, preferred_element_type=jnp.float32).reshape(3, o, depth)


def bias_tap(grads, cols, start, count):
    ones = jnp.ones((8, count * cols), jnp.bfloat16)
    return lax.dot_general(
        ones, grads[1, :, lanes(start, cols, count)], NT, preferred_element_type=jnp.float32
    )


def late_row(block, n_f):
    return block * n_f + jnp.where(block > 0, 0, n_f - 1)


def early_row(block, n_f):
    return block * n_f + jnp.where(block > 0, 1, 0)


def gather_kernel(
    n_f, n_s,
    image, weight, bias_in, cotangent,
    rows, grads, gw_own, gb_own, out,
    w, bias, cot, part, peer, act,
    load_sem, ready_z, ready_x, row_send, row_recv, x_send, sum_send, sum_recv,
    g_send, g_recv, h_send, h_recv, out_send, out_recv, cot_send, cot_recv,
):
    p, s, c = lax.axis_index("filt"), lax.axis_index("sp"), lax.axis_index("in")
    sibling = 1 - c
    cols, depth = rows.shape[1], rows.shape[2]
    o = w.shape[2]
    half_c = out.shape[1]
    total = n_f * n_s
    first = s * n_f
    last = n_f - 1
    x_peers = [lax.rem(s + d, n_s) for d in range(1, n_s)]
    pair = n_s == 2
    other = 1 - s
    low = p < n_f // 2
    dist = jnp.where(low, p, last - p)
    early = (low & (s == 0)) | ((p >= n_f // 2) & (s > 0))
    late = (low & (s > 0)) | ((p >= n_f // 2) & (s == 0))
    bound = jnp.where(s == 0, n_f, -1)
    own_bound = jnp.where(s == 0, last, 0)
    bound_at = jnp.maximum(last - dist, jnp.maximum(dist + 1, 2))

    load_row = pltpu.make_async_copy(image.at[0], rows.at[1 + first + p], load_sem.at[0])
    load_w = pltpu.make_async_copy(
        weight.at[:, :, :, pl.ds(pl.multiple_of(c * depth, depth), depth)], w, load_sem.at[1]
    )
    load_cot = pltpu.make_async_copy(cotangent, cot.at[pl.ds(1, n_f)], load_sem.at[2])
    load_bias = pltpu.make_async_copy(bias_in, bias, load_sem.at[3])
    load_row.start()
    load_w.start()
    load_cot.start()
    load_bias.start()

    barrier = pltpu.get_barrier_semaphore()

    @pl.when(p < last)
    def _():
        pl.semaphore_signal(barrier, 1, device_id={"filt": p + 1}, device_id_type=MESH)

    for peer_s in x_peers:
        @pl.when(peer_s > s)
        def _():
            pl.semaphore_signal(barrier, 1, device_id={"sp": peer_s}, device_id_type=MESH)

    pl.semaphore_signal(barrier, 1, device_id={"in": sibling}, device_id_type=MESH)
    pl.semaphore_wait(barrier, 1 + s + jnp.where(p > 0, 1, 0))

    piece = cols // 2

    def row_copy(q, h, way, where, send):
        slot = rows.at[1 + q, pl.ds(h * piece, piece)]
        return pltpu.make_async_remote_copy(
            src_ref=slot, dst_ref=slot, send_sem=send, recv_sem=row_recv.at[q, h],
            device_id={way: where}, device_id_type=MESH,
        )

    def to_right(q, h):
        return row_copy(q, h, "filt", p + 1, row_send.at[0, q, h])

    def to_left(q, h):
        return row_copy(q, h, "filt", p - 1, row_send.at[1, q, h])

    def to_x(q, h, d):
        return row_copy(first + q, h, "sp", x_peers[d], x_send.at[d, q, h])

    def wait_row(q, h):
        row_copy(q, h, "filt", p, row_send.at[0, 0, 0]).wait_recv()

    def crosses(q, h):
        return ((q > 0) & (q < last)) | (q == p) | (h == 0)

    def pass_on(q, h, right, left):
        if right:
            @pl.when(p < last)
            def _():
                to_right(first + q, h).start()
        if left:
            @pl.when(p > 0)
            def _():
                to_left(first + q, h).start()

        @pl.when(crosses(q, h))
        def _():
            for d in range(n_s - 1):
                to_x(q, h, d).start()

    def own_copy(h, way, where, send):
        place = pl.ds(h * piece, piece)
        return pltpu.make_async_remote_copy(
            src_ref=image.at[0, place], dst_ref=rows.at[1 + first + p, place],
            send_sem=send, recv_sem=row_recv.at[first + p, h],
            device_id={way: where}, device_id_type=MESH,
        )

    def own_to_x(up):
        for d in range(n_s - 1):
            @pl.when((x_peers[d] > s) if up else (x_peers[d] < s))
            def _():
                for h in range(2):
                    own_copy(h, "sp", x_peers[d], x_send.at[d, p, h]).start()

    @pl.when(p > 0)
    def _():
        for h in range(2):
            own_copy(h, "filt", p - 1, row_send.at[1, first + p, h]).start()
        pl.semaphore_signal(ready_z, 1, device_id={"filt": p - 1}, device_id_type=MESH)

    own_to_x(False)
    for peer_s in x_peers:
        @pl.when(peer_s < s)
        def _():
            pl.semaphore_signal(ready_x, 1, device_id={"sp": peer_s}, device_id_type=MESH)

    @pl.when(p < last)
    def _():
        pl.semaphore_wait(ready_z, 1)
        for h in range(2):
            own_copy(h, "filt", p + 1, row_send.at[0, first + p, h]).start()

    @pl.when(s < n_s - 1)
    def _():
        pl.semaphore_wait(ready_x, n_s - 1 - s)

    own_to_x(True)
    load_row.wait()

    zero = jnp.zeros((cols, depth), rows.dtype)
    rows[0] = zero
    rows[total + 1] = zero

    @pl.loop(0, n_f + 2)
    def _(r):
        part[r] = jnp.zeros((o, cols), jnp.float32)

    load_w.wait()

    def add_tap(q, a, r):
        sums = lax.dot_general(
            w[a].reshape(3 * o, depth), rows[1 + q], NT, preferred_element_type=jnp.float32
        )
        part[r + 1] += shift_cols(sums[:o], -1) + sums[o:2 * o] + shift_cols(sums[2 * o:], 1)

    def add_row(q):
        sums = lax.dot_general(
            w[...].reshape(9 * o, depth), rows[1 + first + q], NT, preferred_element_type=jnp.float32
        )
        for a in range(3):
            left, middle, right = (sums[(3 * a + b) * o:(3 * a + b + 1) * o] for b in range(3))
            part[q - a + 2] += shift_cols(left, -1) + middle + shift_cols(right, 1)

    def sum_copy(r):
        return pltpu.make_async_remote_copy(
            src_ref=part.at[r + 1], dst_ref=peer.at[r + 1],
            send_sem=sum_send.at[r + 1], recv_sem=sum_recv.at[r + 1],
            device_id={"in": sibling}, device_id_type=MESH,
        )

    def out_copy(r):
        return pltpu.make_async_remote_copy(
            src_ref=act.at[r, :, pl.ds(pl.multiple_of(c * half_c, half_c), half_c)],
            dst_ref=out.at[pl.ds(pl.multiple_of(p * o, o), o), :],
            send_sem=out_send.at[r], recv_sem=out_recv.at[p],
            device_id={"filt": r}, device_id_type=MESH,
        )

    own_out = pltpu.make_async_copy(
        act.at[p, :, pl.ds(pl.multiple_of(c * half_c, half_c), half_c)],
        out.at[pl.ds(pl.multiple_of(p * o, o), o), :],
        load_sem.at[0],
    )

    half_o = o // 2

    def g_half(q, core):
        return grads.at[1, pl.ds(pl.multiple_of(core * half_o, half_o), half_o), lanes(q, cols)]

    def g_copy(q, d):
        place = g_half(q, c)
        return pltpu.make_async_remote_copy(
            src_ref=place, dst_ref=place, send_sem=g_send.at[d, q], recv_sem=g_recv.at[q],
            device_id={"sp": x_peers[d]}, device_id_type=MESH,
        )

    def h_copy(q, core):
        place = g_half(q, core)
        return pltpu.make_async_remote_copy(
            src_ref=place, dst_ref=place, send_sem=h_send.at[q], recv_sem=h_recv.at[q],
            device_id={"in": sibling}, device_id_type=MESH,
        )

    def half(place, core):
        return place.at[pl.ds(pl.multiple_of(core * half_o, half_o), half_o)]

    def cot_copy():
        return pltpu.make_async_remote_copy(
            src_ref=half(cotangent.at[own_bound], c),
            dst_ref=half(cot.at[jnp.where(s == 0, 0, n_f + 1)], c),
            send_sem=cot_send.at[0], recv_sem=cot_recv.at[0],
            device_id={"sp": other}, device_id_type=MESH,
        )

    def cot_share(core):
        place = half(cot.at[bound + 1], core)
        return pltpu.make_async_remote_copy(
            src_ref=place, dst_ref=place, send_sem=cot_send.at[1], recv_sem=cot_recv.at[1],
            device_id={"in": sibling}, device_id_type=MESH,
        )

    def done_at(r):
        low = jnp.where(s == 0, jnp.maximum(p, 1), jnp.maximum(p, n_f - p))
        high = jnp.where(
            s == n_s - 1, jnp.maximum(last - p, 1), jnp.maximum(last - p, p + 1)
        )
        return jnp.where(r == 0, low, jnp.where(r == last, high, jnp.abs(r - p) + 1))

    def sends_grad(r):
        return early | (r != own_bound) if pair else r >= 0

    def activate(r):
        sum_copy(r).wait_recv()
        bias_all = jnp.broadcast_to(bias[...], (cols, o)).T
        shifted = part[r + 1] + peer[r + 1] + bias_all
        sig = jax.nn.sigmoid(shifted)
        slope = sig * (1.0 + shifted * (1.0 - sig))
        grad = (cot[r + 1].astype(jnp.float32) * slope).astype(jnp.bfloat16)
        grads[1, :, lanes(first + r, cols)] = grad
        return grad, (shifted * sig).astype(jnp.bfloat16)

    def finish(r):
        grad, value = activate(r)
        act[r] = value

        @pl.when(sends_grad(r))
        def _():
            for d in range(n_s - 1):
                g_copy(first + r, d).start()

        send_out(r)
        store_shifts(grads, lanes(first + r, cols), grad)

    def finish_bound():
        grad, _ = activate(bound)
        store_shifts(grads, lanes(first + bound, cols), grad)

    def send_out(r):
        @pl.when(r == p)
        def _():
            own_out.start()

        @pl.when(r != p)
        def _():
            out_copy(r).start()

    add_row(p)
    load_cot.wait()
    load_bias.wait()

    def relay(t):
        @pl.when(t == p + 1)
        def _():
            for block in x_peers:
                wait_row(block * n_f, 1)

                @pl.when(p < last)
                def _():
                    to_right(block * n_f, 1).start()

                wait_row(block * n_f, 0)

        @pl.when(t == n_f - p)
        def _():
            for block in x_peers:
                wait_row(block * n_f + last, 1)

                @pl.when(p > 0)
                def _():
                    to_left(block * n_f + last, 1).start()

                wait_row(block * n_f + last, 0)

    def add_edges(t):
        if pair:
            tap = jnp.where(s == 0, 2, 0)
            edge = jnp.where(s == 0, first + n_f, first - 1)
            after = jnp.where(s == 0, first + n_f + 1, first - 2)

            @pl.when(t == jnp.where(early, dist + 1, n_f - dist))
            def _():
                add_tap(edge, tap, own_bound)

            @pl.when(early & (t == dist + 1))
            def _():
                add_tap(edge, 1, bound)

            @pl.when(early & (t == jnp.maximum(dist + 1, 2)))
            def _():
                for h in range(2):
                    wait_row(after, h)
                add_tap(after, tap, bound)

            return

        @pl.when((t == p + 1) & (s < n_s - 1))
        def _():
            add_tap(first + n_f, 2, last)

        @pl.when((t == n_f - p) & (s > 0))
        def _():
            add_tap(first - 1, 0, 0)

    def start_sums(t):
        @pl.loop(0, n_f)
        def _(r):
            @pl.when(done_at(r) == t)
            def _():
                sum_copy(r).start()

        if pair:
            @pl.when(early & (t == bound_at))
            def _():
                sum_copy(bound).start()

    def finish_rows(t):
        @pl.loop(0, n_f)
        def _(r):
            @pl.when(done_at(r) == t)
            def _():
                finish(r)

    @pl.loop(1, n_f)
    def _(t):
        for h in range(2):
            @pl.when(p - t >= 0)
            def _():
                wait_row(first + p - t, h)
                pass_on(p - t, h, True, False)

            @pl.when(p + t < n_f)
            def _():
                wait_row(first + p + t, h)
                pass_on(p + t, h, False, True)

        relay(t)

        @pl.when(p - t >= 0)
        def _():
            add_row(p - t)

        @pl.when(p + t < n_f)
        def _():
            add_row(p + t)

        add_edges(t)
        start_sums(t)

        if pair:
            @pl.when(late & (t == n_f - 2))
            def _():
                cot_copy().start()

        finish_rows(t)

    own_start = early_row(s, n_f)

    def own_rows(a):
        gw_own[3 * a:3 * a + 3] = rows_tap(rows, grads, a, own_start, n_f - 1)

    def add_rows(a, start, count):
        gw_own[3 * a:3 * a + 3] += rows_tap(rows, grads, a, start, count)

    def add_bias(start, count):
        gb_own[...] += bias_tap(grads, cols, start, count)

    def share_grad(q):
        g_copy(q, 0).wait_recv()
        h_copy(q, c).start()

    def take_grad(q):
        h_copy(q, sibling).wait_recv()
        place = lanes(q, cols)
        store_shifts(grads, place, grads[1, :, place])

    def tail_of_pair():
        near = n_f // 2

        def place(k):
            return other * n_f + jnp.where(low, k, last - k)

        @pl.when(early)
        def _():
            cot_copy().wait_recv()
            cot_share(c).start()

        @pl.when(late)
        def _():
            relay(n_f)
            add_edges(n_f)
            start_sums(n_f)

        own_rows(0)
        own_rows(1)

        @pl.when(early)
        def _():
            cot_share(sibling).wait_recv()
            finish_bound()

        finish_rows(n_f)

        @pl.when(late)
        def _():
            share_grad(place(0))

        @pl.loop(1, near)
        def _(k):
            share_grad(place(k))

        own_rows(2)
        gb_own[...] = bias_tap(grads, cols, own_start, n_f - 1)

        @pl.when(late)
        def _():
            for h in range(2):
                wait_row(place(1), h)
            take_grad(place(0))

        @pl.when(early)
        def _():
            relay(n_f)

        @pl.loop(2, last)
        def _(k):
            for h in range(2):
                wait_row(place(k), h)

        @pl.loop(1, near)
        def _(k):
            take_grad(place(k))

        some = jnp.where(
            early, jnp.where(low, last, n_f - near + 1), jnp.where(low, 0, 2 * n_f - near)
        )
        one = jnp.where(
            early, jnp.where(low, n_f + near - 1, n_f - near), jnp.where(low, n_f, last)
        )
        for a in range(3):
            add_rows(a, some, near)
        for a in range(3):
            add_rows(a, one, 1)
        add_bias(some, near)
        add_bias(one, 1)

        @pl.loop(near, n_f)
        def _(k):
            share_grad(place(k))

        @pl.loop(near, n_f)
        def _(k):
            take_grad(place(k))

    def tail_of_many():
        relay(n_f)
        add_edges(n_f)
        start_sums(n_f)
        finish_rows(n_f)
        for a in range(3):
            own_rows(a)
        gb_own[...] = bias_tap(grads, cols, own_start, n_f - 1)

        for block in x_peers:
            start = early_row(block, n_f)

            @pl.loop(1, last)
            def _(q):
                for h in range(2):
                    wait_row(block * n_f + q, h)

            @pl.loop(0, n_f - 1)
            def _(q):
                share_grad(start + q)

            @pl.loop(0, n_f - 1)
            def _(q):
                take_grad(start + q)

            for a in range(3):
                add_rows(a, start, n_f - 1)

            add_bias(start, n_f - 1)

        for block in x_peers:
            share_grad(late_row(block, n_f))
            take_grad(late_row(block, n_f))

    if pair:
        tail_of_pair()
    else:
        tail_of_many()

    @pl.loop(0, n_f)
    def _(r):
        sum_copy(r).wait_send()

        @pl.when(r == p)
        def _():
            own_out.wait()

        @pl.when(r != p)
        def _():
            out_copy(r).wait_send()
            pltpu.make_async_remote_copy(
                src_ref=act.at[r, :, pl.ds(0, half_c)],
                dst_ref=out.at[pl.ds(pl.multiple_of(r * o, o), o), :],
                send_sem=out_send.at[r], recv_sem=out_recv.at[r],
                device_id={"filt": r}, device_id_type=MESH,
            ).wait_recv()

        for d in range(n_s - 1):
            @pl.when(sends_grad(r))
            def _():
                g_copy(first + r, d).wait_send()

            for h in range(2):
                @pl.when(crosses(r, h))
                def _():
                    to_x(r, h, d).wait_send()

        @pl.when((r <= p) & (p < last))
        def _():
            for h in range(2):
                to_right(first + r, h).wait_send()

        @pl.when((r >= p) & (p > 0))
        def _():
            for h in range(2):
                to_left(first + r, h).wait_send()

    for block in x_peers:
        @pl.loop(0, n_f)
        def _(q):
            if pair:
                @pl.when(late | (q != jnp.where(low, 0, last)))
                def _():
                    h_copy(block * n_f + q, c).wait_send()
            else:
                h_copy(block * n_f + q, c).wait_send()

        @pl.when(p < last)
        def _():
            to_right(block * n_f, 1).wait_send()

        @pl.when(p > 0)
        def _():
            to_left(block * n_f + last, 1).wait_send()

    if pair:
        @pl.when(early)
        def _():
            sum_copy(bound).wait_send()
            cot_share(c).wait_send()

        @pl.when(late)
        def _():
            cot_copy().wait_send()


def finish_kernel(n_f, n_s, rows, grads, gw_own, gb_own, out_in, gw, gb, out, total, sem, out_sem):
    cols = rows.shape[1]
    out_copy = pltpu.make_async_copy(out_in, out.at[0], out_sem)
    out_copy.start()

    if n_s == 2:
        p, s = lax.axis_index("filt"), lax.axis_index("sp")
        near = n_f // 2
        late = [((1 - s) * n_f + jnp.where(p < near, near, 0), n_f - near)]
    else:
        late = [(n_f - 1, 2)] + [(block * n_f, 1) for block in range(2, n_s)]

    def gw_copy(a):
        return pltpu.make_async_copy(total.at[a], gw.at[a], sem.at[a])

    for a in range(3):
        value = gw_own[3 * a:3 * a + 3]
        for start, count in late:
            value = value + rows_tap(rows, grads, a, start, count)
        total[a] = value
        gw_copy(a).start()

    bias = gb_own[...]
    for start, count in late:
        bias = bias + bias_tap(grads, cols, start, count)
    gb[...] = bias[:1]

    for a in range(3):
        gw_copy(a).wait()

    out_copy.wait()


def on_device(image, weight, bias, cotangent):
    n_f, n_s, n_in = (lax.axis_size(name) for name in ("filt", "sp", "in"))
    row_count, o, cols = cotangent.shape
    depth = image.shape[2]
    total = n_f * n_s
    any_space = pl.BlockSpec(memory_space=pl.ANY)
    vmem = pl.BlockSpec(memory_space=pltpu.VMEM)
    hbm = pl.BlockSpec(memory_space=pltpu.HBM)
    dma = pltpu.SemaphoreType.DMA
    between = pl.pallas_call(
        functools.partial(gather_kernel, n_f, n_s),
        out_shape=(
            pltpu.VMEM((total + 2, cols, depth), jnp.bfloat16),
            pltpu.VMEM((3, o, total * cols), jnp.bfloat16),
            pltpu.VMEM((9, o, depth), jnp.float32),
            pltpu.VMEM((8, o), jnp.float32),
            pltpu.VMEM((n_f * o, cols // n_in), jnp.bfloat16),
        ),
        in_specs=[hbm, hbm, hbm, hbm],
        out_specs=(vmem,) * 5,
        scratch_shapes=[
            pltpu.VMEM((3, 3, o, depth), jnp.bfloat16),
            pltpu.VMEM((1, o), jnp.float32),
            pltpu.VMEM((n_f + 2, o, cols), jnp.bfloat16),
            pltpu.VMEM((n_f + 2, o, cols), jnp.float32),
            pltpu.VMEM((n_f + 2, o, cols), jnp.float32),
            pltpu.VMEM((n_f, o, cols), jnp.bfloat16),
            dma((4,)),
            pltpu.SemaphoreType.REGULAR,
            pltpu.SemaphoreType.REGULAR,
            dma((2, total, 2)),
            dma((total, 2)),
            dma((n_s - 1, n_f, 2)),
            dma((n_f + 2,)),
            dma((n_f + 2,)),
            dma((n_s - 1, total)),
            dma((total,)),
            dma((total,)),
            dma((total,)),
            dma((n_f,)),
            dma((n_f,)),
            dma((2,)),
            dma((2,)),
        ],
        compiler_params=pltpu.CompilerParams(
            collective_id=0, has_side_effects=True, vmem_limit_bytes=24 * 1024 * 1024
        ),
        name="gather",
    )(*(
        pltpu.with_memory_space_constraint(x, pltpu.HBM)
        for x in (image, weight, bias.reshape(1, o), cotangent)
    ))
    grad_weight, grad_bias, output = pl.pallas_call(
        functools.partial(finish_kernel, n_f, n_s),
        out_shape=(
            jax.ShapeDtypeStruct((3, 3, o, depth), jnp.float32),
            jax.ShapeDtypeStruct((1, o), jnp.float32),
            jax.ShapeDtypeStruct((1, n_f * o, cols // n_in), jnp.bfloat16),
        ),
        in_specs=[vmem] * 5,
        out_specs=(any_space, vmem, any_space),
        scratch_shapes=[
            pltpu.VMEM((3, 3, o, depth), jnp.float32),
            dma((3,)),
            dma(()),
        ],
        compiler_params=pltpu.CompilerParams(vmem_limit_bytes=20 * 1024 * 1024),
        name="finish",
    )(*between)
    return (output, grad_weight, grad_bias.reshape(o))


def solution(mesh):
    placed = (
        P(("groups", "sp", "filt"), None, "in"),
        P(None, None, "filt", None),
        P("filt"),
        P(("groups", "sp"), "filt", None),
    )
    return jax.shard_map(
        on_device,
        mesh=mesh,
        in_specs=placed,
        out_specs=(
            P(("groups", "sp", "filt"), None, "in"),
            P("groups", None, "filt", "in"),
            P(("groups", "filt")),
        ),
        check_vma=False,
    )
```

```python
import functools

import jax
import jax.numpy as jnp
from jax import lax
from jax.experimental import pallas as pl
from jax.experimental.pallas import tpu as pltpu
from jax.sharding import PartitionSpec as P

MESH = pl.DeviceIdType.MESH
NT = (((1,), (1,)), ((), ()))


def shift_cols(value, by):
    cols = value.shape[1]
    col = lax.broadcasted_iota(jnp.int32, value.shape, 1)
    if by < 0:
        return jnp.where(col == 0, 0.0, pltpu.roll(value, 1, 1))
    return jnp.where(col == cols - 1, 0.0, pltpu.roll(value, cols - 1, 1))


def lanes(q, cols, count=1):
    return pl.ds(pl.multiple_of(q * cols, cols), count * cols)


def store_shifts(grads, place, grad):
    wide = grad.astype(jnp.float32)
    grads[0, :, place] = shift_cols(wide, 1).astype(jnp.bfloat16)
    grads[2, :, place] = shift_cols(wide, -1).astype(jnp.bfloat16)


def rows_tap(rows, grads, a, start, count):
    cols, depth = rows.shape[1], rows.shape[2]
    o = grads.shape[1]
    window = rows[pl.ds(start + a, count)].reshape(count * cols, depth)
    left = grads[:, :, lanes(start, cols, count)].reshape(3 * o, count * cols)
    return jnp.dot(left, window, preferred_element_type=jnp.float32).reshape(3, o, depth)


def bias_tap(grads, cols, start, count):
    ones = jnp.ones((8, count * cols), jnp.bfloat16)
    return lax.dot_general(
        ones, grads[1, :, lanes(start, cols, count)], NT, preferred_element_type=jnp.float32
    )


def late_row(block, n_f):
    return block * n_f + jnp.where(block > 0, 0, n_f - 1)


def early_row(block, n_f):
    return block * n_f + jnp.where(block > 0, 1, 0)


def gather_kernel(
    n_f, n_s,
    image, weight, bias_in, cotangent,
    rows, grads, gw_own, gb_own, out,
    w, bias, cot, part, peer, act,
    load_sem, ready_z, ready_x, row_send, row_recv, x_send, sum_send, sum_recv,
    g_send, g_recv, h_send, h_recv, out_send, out_recv, cot_send, cot_recv,
):
    p, s, c = lax.axis_index("filt"), lax.axis_index("sp"), lax.axis_index("in")
    sibling = 1 - c
    cols, depth = rows.shape[1], rows.shape[2]
    o = w.shape[2]
    half_c = out.shape[1]
    total = n_f * n_s
    first = s * n_f
    last = n_f - 1
    x_peers = [lax.rem(s + d, n_s) for d in range(1, n_s)]
    pair = n_s == 2
    other = 1 - s
    low = p < n_f // 2
    dist = jnp.where(low, p, last - p)
    early = (low & (s == 0)) | ((p >= n_f // 2) & (s > 0))
    late = (low & (s > 0)) | ((p >= n_f // 2) & (s == 0))
    bound = jnp.where(s == 0, n_f, -1)
    own_bound = jnp.where(s == 0, last, 0)
    bound_at = jnp.maximum(last - dist, jnp.maximum(dist + 1, 2))
    near = n_f // 2

    def down_row(block):
        return jnp.where(block == 0, last - 1, last)

    def up_row(block):
        return jnp.where(block == 0, 0, 1)

    def relayed(q, block):
        down, up = down_row(block), up_row(block)
        return ((q == down) & (p < down)) | ((q == up) & (p > up))

    load_row = pltpu.make_async_copy(image.at[0], rows.at[1 + first + p], load_sem.at[0])
    load_w = pltpu.make_async_copy(
        weight.at[:, :, :, pl.ds(pl.multiple_of(c * depth, depth), depth)], w, load_sem.at[1]
    )
    load_cot = pltpu.make_async_copy(cotangent, cot.at[pl.ds(1, n_f)], load_sem.at[2])
    load_bias = pltpu.make_async_copy(bias_in, bias, load_sem.at[3])
    load_row.start()
    load_w.start()
    load_cot.start()
    load_bias.start()

    barrier = pltpu.get_barrier_semaphore()

    @pl.when(p < last)
    def _():
        pl.semaphore_signal(barrier, 1, device_id={"filt": p + 1}, device_id_type=MESH)

    for peer_s in x_peers:
        @pl.when(peer_s > s)
        def _():
            pl.semaphore_signal(barrier, 1, device_id={"sp": peer_s}, device_id_type=MESH)

    pl.semaphore_signal(barrier, 1, device_id={"in": sibling}, device_id_type=MESH)
    pl.semaphore_wait(barrier, 1 + s + jnp.where(p > 0, 1, 0))

    piece = cols // 2

    def row_copy(q, h, way, where, send):
        slot = rows.at[1 + q, pl.ds(h * piece, piece)]
        return pltpu.make_async_remote_copy(
            src_ref=slot, dst_ref=slot, send_sem=send, recv_sem=row_recv.at[q, h],
            device_id={way: where}, device_id_type=MESH,
        )

    def to_right(q, h):
        return row_copy(q, h, "filt", p + 1, row_send.at[0, q, h])

    def to_left(q, h):
        return row_copy(q, h, "filt", p - 1, row_send.at[1, q, h])

    def to_x(q, h, d):
        return row_copy(first + q, h, "sp", x_peers[d], x_send.at[d, q, h])

    def wait_row(q, h):
        row_copy(q, h, "filt", p, row_send.at[0, 0, 0]).wait_recv()

    def crosses(q, h):
        if pair:
            return jnp.logical_not(relayed(q, s))
        return ((q > 0) & (q < last)) | (q == p) | (h == 0)

    def pass_on(q, h, right, left):
        if right:
            @pl.when(p < last)
            def _():
                to_right(first + q, h).start()
        if left:
            @pl.when(p > 0)
            def _():
                to_left(first + q, h).start()

        @pl.when(crosses(q, h))
        def _():
            for d in range(n_s - 1):
                to_x(q, h, d).start()

    def own_copy(h, way, where, send):
        place = pl.ds(h * piece, piece)
        return pltpu.make_async_remote_copy(
            src_ref=image.at[0, place], dst_ref=rows.at[1 + first + p, place],
            send_sem=send, recv_sem=row_recv.at[first + p, h],
            device_id={way: where}, device_id_type=MESH,
        )

    def own_to_x(up):
        for d in range(n_s - 1):
            @pl.when((x_peers[d] > s) if up else (x_peers[d] < s))
            def _():
                for h in range(2):
                    own_copy(h, "sp", x_peers[d], x_send.at[d, p, h]).start()

    @pl.when(p > 0)
    def _():
        for h in range(2):
            own_copy(h, "filt", p - 1, row_send.at[1, first + p, h]).start()
        pl.semaphore_signal(ready_z, 1, device_id={"filt": p - 1}, device_id_type=MESH)

    own_to_x(False)
    for peer_s in x_peers:
        @pl.when(peer_s < s)
        def _():
            pl.semaphore_signal(ready_x, 1, device_id={"sp": peer_s}, device_id_type=MESH)

    @pl.when(p < last)
    def _():
        pl.semaphore_wait(ready_z, 1)
        for h in range(2):
            own_copy(h, "filt", p + 1, row_send.at[0, first + p, h]).start()

    @pl.when(s < n_s - 1)
    def _():
        pl.semaphore_wait(ready_x, n_s - 1 - s)

    own_to_x(True)
    load_row.wait()

    zero = jnp.zeros((cols, depth), rows.dtype)
    rows[0] = zero
    rows[total + 1] = zero

    @pl.loop(0, n_f + 2)
    def _(r):
        part[r] = jnp.zeros((o, cols), jnp.float32)

    load_w.wait()

    if pair:
        @pl.loop(0, 9)
        def _(k):
            gw_own[k] = jnp.zeros((o, depth), jnp.float32)

        gb_own[...] = jnp.zeros(gb_own.shape, jnp.float32)

    def add_tap(q, a, r):
        sums = lax.dot_general(
            w[a].reshape(3 * o, depth), rows[1 + q], NT, preferred_element_type=jnp.float32
        )
        part[r + 1] += shift_cols(sums[:o], -1) + sums[o:2 * o] + shift_cols(sums[2 * o:], 1)

    def add_row(q):
        sums = lax.dot_general(
            w[...].reshape(9 * o, depth), rows[1 + first + q], NT, preferred_element_type=jnp.float32
        )
        for a in range(3):
            left, middle, right = (sums[(3 * a + b) * o:(3 * a + b + 1) * o] for b in range(3))
            part[q - a + 2] += shift_cols(left, -1) + middle + shift_cols(right, 1)

    def sum_copy(r):
        return pltpu.make_async_remote_copy(
            src_ref=part.at[r + 1], dst_ref=peer.at[r + 1],
            send_sem=sum_send.at[r + 1], recv_sem=sum_recv.at[r + 1],
            device_id={"in": sibling}, device_id_type=MESH,
        )

    def out_copy(r):
        return pltpu.make_async_remote_copy(
            src_ref=act.at[r, :, pl.ds(pl.multiple_of(c * half_c, half_c), half_c)],
            dst_ref=out.at[pl.ds(pl.multiple_of(p * o, o), o), :],
            send_sem=out_send.at[r], recv_sem=out_recv.at[p],
            device_id={"filt": r}, device_id_type=MESH,
        )

    own_out = pltpu.make_async_copy(
        act.at[p, :, pl.ds(pl.multiple_of(c * half_c, half_c), half_c)],
        out.at[pl.ds(pl.multiple_of(p * o, o), o), :],
        load_sem.at[0],
    )

    half_o = o // 2

    def g_half(q, core):
        return grads.at[1, pl.ds(pl.multiple_of(core * half_o, half_o), half_o), lanes(q, cols)]

    def g_copy(q, d):
        place = g_half(q, c)
        return pltpu.make_async_remote_copy(
            src_ref=place, dst_ref=place, send_sem=g_send.at[d, q], recv_sem=g_recv.at[q],
            device_id={"sp": x_peers[d]}, device_id_type=MESH,
        )

    def h_copy(q, core):
        place = g_half(q, core)
        return pltpu.make_async_remote_copy(
            src_ref=place, dst_ref=place, send_sem=h_send.at[q], recv_sem=h_recv.at[q],
            device_id={"in": sibling}, device_id_type=MESH,
        )

    def half(place, core):
        return place.at[pl.ds(pl.multiple_of(core * half_o, half_o), half_o)]

    def cot_copy():
        return pltpu.make_async_remote_copy(
            src_ref=half(cotangent.at[own_bound], c),
            dst_ref=half(cot.at[jnp.where(s == 0, 0, n_f + 1)], c),
            send_sem=cot_send.at[0], recv_sem=cot_recv.at[0],
            device_id={"sp": other}, device_id_type=MESH,
        )

    def cot_share(core):
        place = half(cot.at[bound + 1], core)
        return pltpu.make_async_remote_copy(
            src_ref=place, dst_ref=place, send_sem=cot_send.at[1], recv_sem=cot_recv.at[1],
            device_id={"in": sibling}, device_id_type=MESH,
        )

    def done_at(r):
        low = jnp.where(s == 0, jnp.maximum(p, 1), jnp.maximum(p, n_f - p))
        high = jnp.where(
            s == n_s - 1, jnp.maximum(last - p, 1), jnp.maximum(last - p, p + 1)
        )
        return jnp.where(r == 0, low, jnp.where(r == last, high, jnp.abs(r - p) + 1))

    def sends_grad(r):
        return early | (r != own_bound) if pair else r >= 0

    def activate(r):
        sum_copy(r).wait_recv()
        bias_all = jnp.broadcast_to(bias[...], (cols, o)).T
        shifted = part[r + 1] + peer[r + 1] + bias_all
        sig = jax.nn.sigmoid(shifted)
        slope = sig * (1.0 + shifted * (1.0 - sig))
        grad = (cot[r + 1].astype(jnp.float32) * slope).astype(jnp.bfloat16)
        grads[1, :, lanes(first + r, cols)] = grad
        return grad, (shifted * sig).astype(jnp.bfloat16)

    def finish(r):
        grad, value = activate(r)
        act[r] = value

        @pl.when(sends_grad(r))
        def _():
            for d in range(n_s - 1):
                g_copy(first + r, d).start()

        send_out(r)
        store_shifts(grads, lanes(first + r, cols), grad)

    def finish_bound():
        grad, _ = activate(bound)
        store_shifts(grads, lanes(first + bound, cols), grad)

    def send_out(r):
        @pl.when(r == p)
        def _():
            own_out.start()

        @pl.when(r != p)
        def _():
            out_copy(r).start()

    add_row(p)
    load_cot.wait()
    load_bias.wait()

    def relay_pair(t):
        down, up = down_row(other), up_row(other)

        @pl.when((p <= down) & (t == jnp.where(p == down, 1, n_f - p)))
        def _():
            for h in range(2):
                wait_row(other * n_f + down, h)

                @pl.when(p > 0)
                def _():
                    to_left(other * n_f + down, h).start()

        @pl.when((p >= up) & (t == jnp.where(p == up, 1, p + 1)))
        def _():
            for h in range(2):
                wait_row(other * n_f + up, h)

                @pl.when(p < last)
                def _():
                    to_right(other * n_f + up, h).start()

    def arrive(q):
        down, up = down_row(other), up_row(other)

        @pl.when(jnp.logical_not(((q == down) & (p <= down)) | ((q == up) & (p >= up))))
        def _():
            for h in range(2):
                wait_row(other * n_f + q, h)

    def relay(t):
        if pair:
            return relay_pair(t)

        @pl.when(t == p + 1)
        def _():
            for block in x_peers:
                wait_row(block * n_f, 1)

                @pl.when(p < last)
                def _():
                    to_right(block * n_f, 1).start()

                wait_row(block * n_f, 0)

        @pl.when(t == n_f - p)
        def _():
            for block in x_peers:
                wait_row(block * n_f + last, 1)

                @pl.when(p > 0)
                def _():
                    to_left(block * n_f + last, 1).start()

                wait_row(block * n_f + last, 0)

    def add_edges(t):
        if pair:
            tap = jnp.where(s == 0, 2, 0)
            edge = jnp.where(s == 0, first + n_f, first - 1)
            after = jnp.where(s == 0, first + n_f + 1, first - 2)

            @pl.when(t == jnp.where(early, dist + 1, n_f - dist))
            def _():
                arrive(edge - other * n_f)
                add_tap(edge, tap, own_bound)

            @pl.when(early & (t == dist + 1))
            def _():
                add_tap(edge, 1, bound)

            @pl.when(early & (t == jnp.maximum(dist + 1, 2)))
            def _():
                arrive(after - other * n_f)
                add_tap(after, tap, bound)

            return

        @pl.when((t == p + 1) & (s < n_s - 1))
        def _():
            add_tap(first + n_f, 2, last)

        @pl.when((t == n_f - p) & (s > 0))
        def _():
            add_tap(first - 1, 0, 0)

    def start_sums(t):
        @pl.loop(0, n_f)
        def _(r):
            @pl.when(done_at(r) == t)
            def _():
                sum_copy(r).start()

        if pair:
            @pl.when(early & (t == bound_at))
            def _():
                sum_copy(bound).start()

    def finish_rows(t):
        @pl.loop(0, n_f)
        def _(r):
            @pl.when(done_at(r) == t)
            def _():
                finish(r)

    own_start = early_row(s, n_f)

    def own_rows(a):
        gw_own[3 * a:3 * a + 3] = rows_tap(rows, grads, a, own_start, n_f - 1)

    def add_rows(a, start, count):
        gw_own[3 * a:3 * a + 3] += rows_tap(rows, grads, a, start, count)

    def add_bias(start, count):
        gb_own[...] += bias_tap(grads, cols, start, count)

    def share_grad(q):
        g_copy(q, 0).wait_recv()
        h_copy(q, c).start()

    def take_grad(q):
        h_copy(q, sibling).wait_recv()
        place = lanes(q, cols)
        store_shifts(grads, place, grads[1, :, place])

    def add_all(start, count):
        for a in range(3):
            add_rows(a, start, count)
        add_bias(start, count)

    def near_rows():
        @pl.when(early)
        def _():
            add_all(first + jnp.where(low, 0, n_f - near), near)

        @pl.when(late)
        def _():
            add_all(first + jnp.where(low, 1, n_f - near), near - 1)

    def tail_of_pair():
        def place(k):
            return other * n_f + jnp.where(low, k, last - k)

        @pl.when(early)
        def _():
            cot_copy().wait_recv()
            cot_share(c).start()

        @pl.when(late)
        def _():
            add_edges(n_f)
            start_sums(n_f)

        add_all(first + jnp.where(low, near, 0), n_f - near)

        @pl.when(early)
        def _():
            share_grad(place(1))
            cot_share(sibling).wait_recv()
            finish_bound()

            @pl.loop(2, last)
            def _(k):
                arrive(place(k) - other * n_f)

        @pl.when(late)
        def _():
            finish_rows(n_f)
            share_grad(place(0))
            share_grad(place(1))
            add_all(first + own_bound, 1)

            @pl.loop(0, last - 1)
            def _(k):
                arrive(place(k) - other * n_f)

            take_grad(place(0))

        @pl.loop(2, near)
        def _(k):
            share_grad(place(k))

        @pl.loop(1, near)
        def _(k):
            take_grad(place(k))

        relay(n_f)
        add_all(other * n_f + jnp.where(low, 0, n_f - near), near)

        @pl.loop(near, n_f)
        def _(k):
            share_grad(place(k))
            take_grad(place(k))

            @pl.when(k < last)
            def _():
                add_all(place(k), 1)

    def tail_of_many():
        relay(n_f)
        add_edges(n_f)
        start_sums(n_f)
        finish_rows(n_f)
        for a in range(3):
            own_rows(a)
        gb_own[...] = bias_tap(grads, cols, own_start, n_f - 1)

        for block in x_peers:
            start = early_row(block, n_f)

            @pl.loop(1, last)
            def _(q):
                for h in range(2):
                    wait_row(block * n_f + q, h)

            @pl.loop(0, n_f - 1)
            def _(q):
                share_grad(start + q)

            @pl.loop(0, n_f - 1)
            def _(q):
                take_grad(start + q)

            for a in range(3):
                add_rows(a, start, n_f - 1)

            add_bias(start, n_f - 1)

        for block in x_peers:
            share_grad(late_row(block, n_f))
            take_grad(late_row(block, n_f))

    @pl.loop(1, n_f)
    def _(t):
        for h in range(2):
            @pl.when(p - t >= 0)
            def _():
                wait_row(first + p - t, h)
                pass_on(p - t, h, True, False)

            @pl.when(p + t < n_f)
            def _():
                wait_row(first + p + t, h)
                pass_on(p + t, h, False, True)

        relay(t)

        @pl.when(p - t >= 0)
        def _():
            add_row(p - t)

        @pl.when(p + t < n_f)
        def _():
            add_row(p + t)

        add_edges(t)
        start_sums(t)

        if pair:
            @pl.when(late & (t == n_f - 2))
            def _():
                cot_copy().start()

        finish_rows(t)

        if pair:
            @pl.when(t == n_f - 2)
            def _():
                near_rows()

    if pair:
        tail_of_pair()
    else:
        tail_of_many()

    @pl.loop(0, n_f)
    def _(r):
        sum_copy(r).wait_send()

        @pl.when(r == p)
        def _():
            own_out.wait()

        @pl.when(r != p)
        def _():
            out_copy(r).wait_send()
            pltpu.make_async_remote_copy(
                src_ref=act.at[r, :, pl.ds(0, half_c)],
                dst_ref=out.at[pl.ds(pl.multiple_of(r * o, o), o), :],
                send_sem=out_send.at[r], recv_sem=out_recv.at[r],
                device_id={"filt": r}, device_id_type=MESH,
            ).wait_recv()

        for d in range(n_s - 1):
            @pl.when(sends_grad(r))
            def _():
                g_copy(first + r, d).wait_send()

            for h in range(2):
                @pl.when(crosses(r, h))
                def _():
                    to_x(r, h, d).wait_send()

        @pl.when((r <= p) & (p < last))
        def _():
            for h in range(2):
                to_right(first + r, h).wait_send()

        @pl.when((r >= p) & (p > 0))
        def _():
            for h in range(2):
                to_left(first + r, h).wait_send()

    if pair:
        @pl.when((p <= down_row(other)) & (p > 0))
        def _():
            for h in range(2):
                to_left(other * n_f + down_row(other), h).wait_send()

        @pl.when((p >= up_row(other)) & (p < last))
        def _():
            for h in range(2):
                to_right(other * n_f + up_row(other), h).wait_send()

    for block in x_peers:
        @pl.loop(0, n_f)
        def _(q):
            if pair:
                @pl.when(late | (q != jnp.where(low, 0, last)))
                def _():
                    h_copy(block * n_f + q, c).wait_send()
            else:
                h_copy(block * n_f + q, c).wait_send()

        if not pair:
            @pl.when(p < last)
            def _():
                to_right(block * n_f, 1).wait_send()

            @pl.when(p > 0)
            def _():
                to_left(block * n_f + last, 1).wait_send()

    if pair:
        @pl.when(early)
        def _():
            sum_copy(bound).wait_send()
            cot_share(c).wait_send()

        @pl.when(late)
        def _():
            cot_copy().wait_send()


def finish_kernel(n_f, n_s, rows, grads, gw_own, gb_own, out_in, gw, gb, out, total, sem, out_sem):
    cols = rows.shape[1]
    out_copy = pltpu.make_async_copy(out_in, out.at[0], out_sem)
    out_copy.start()

    if n_s == 2:
        p, s = lax.axis_index("filt"), lax.axis_index("sp")
        late = [((1 - s) * n_f + jnp.where(p < n_f // 2, n_f - 1, 0), 1)]
    else:
        late = [(n_f - 1, 2)] + [(block * n_f, 1) for block in range(2, n_s)]

    def gw_copy(k):
        return pltpu.make_async_copy(total.at[k], gw.at[k // 3, k % 3], sem.at[k])

    bias = gb_own[...]
    for start, count in late:
        bias = bias + bias_tap(grads, cols, start, count)
    gb[...] = bias[:1]

    for a in range(3):
        value = gw_own[3 * a:3 * a + 3]
        for start, count in late:
            value = value + rows_tap(rows, grads, a, start, count)
        for b in range(3):
            total[3 * a + b] = value[b]
            gw_copy(3 * a + b).start()

    for k in range(9):
        gw_copy(k).wait()

    out_copy.wait()


def on_device(image, weight, bias, cotangent):
    n_f, n_s, n_in = (lax.axis_size(name) for name in ("filt", "sp", "in"))
    row_count, o, cols = cotangent.shape
    depth = image.shape[2]
    total = n_f * n_s
    any_space = pl.BlockSpec(memory_space=pl.ANY)
    vmem = pl.BlockSpec(memory_space=pltpu.VMEM)
    hbm = pl.BlockSpec(memory_space=pltpu.HBM)
    dma = pltpu.SemaphoreType.DMA
    between = pl.pallas_call(
        functools.partial(gather_kernel, n_f, n_s),
        out_shape=(
            pltpu.VMEM((total + 2, cols, depth), jnp.bfloat16),
            pltpu.VMEM((3, o, total * cols), jnp.bfloat16),
            pltpu.VMEM((9, o, depth), jnp.float32),
            pltpu.VMEM((8, o), jnp.float32),
            pltpu.VMEM((n_f * o, cols // n_in), jnp.bfloat16),
        ),
        in_specs=[hbm, hbm, hbm, hbm],
        out_specs=(vmem,) * 5,
        scratch_shapes=[
            pltpu.VMEM((3, 3, o, depth), jnp.bfloat16),
            pltpu.VMEM((1, o), jnp.float32),
            pltpu.VMEM((n_f + 2, o, cols), jnp.bfloat16),
            pltpu.VMEM((n_f + 2, o, cols), jnp.float32),
            pltpu.VMEM((n_f + 2, o, cols), jnp.float32),
            pltpu.VMEM((n_f, o, cols), jnp.bfloat16),
            dma((4,)),
            pltpu.SemaphoreType.REGULAR,
            pltpu.SemaphoreType.REGULAR,
            dma((2, total, 2)),
            dma((total, 2)),
            dma((n_s - 1, n_f, 2)),
            dma((n_f + 2,)),
            dma((n_f + 2,)),
            dma((n_s - 1, total)),
            dma((total,)),
            dma((total,)),
            dma((total,)),
            dma((n_f,)),
            dma((n_f,)),
            dma((2,)),
            dma((2,)),
        ],
        compiler_params=pltpu.CompilerParams(
            collective_id=0, has_side_effects=True, vmem_limit_bytes=24 * 1024 * 1024
        ),
        name="gather",
    )(*(
        pltpu.with_memory_space_constraint(x, pltpu.HBM)
        for x in (image, weight, bias.reshape(1, o), cotangent)
    ))
    grad_weight, grad_bias, output = pl.pallas_call(
        functools.partial(finish_kernel, n_f, n_s),
        out_shape=(
            jax.ShapeDtypeStruct((3, 3, o, depth), jnp.float32),
            jax.ShapeDtypeStruct((1, o), jnp.float32),
            jax.ShapeDtypeStruct((1, n_f * o, cols // n_in), jnp.bfloat16),
        ),
        in_specs=[vmem] * 5,
        out_specs=(any_space, vmem, any_space),
        scratch_shapes=[
            pltpu.VMEM((9, o, depth), jnp.float32),
            dma((9,)),
            dma(()),
        ],
        compiler_params=pltpu.CompilerParams(vmem_limit_bytes=20 * 1024 * 1024),
        name="finish",
    )(*between)
    return (output, grad_weight, grad_bias.reshape(o))


def solution(mesh):
    placed = (
        P(("groups", "sp", "filt"), None, "in"),
        P(None, None, "filt", None),
        P("filt"),
        P(("groups", "sp"), "filt", None),
    )
    return jax.shard_map(
        on_device,
        mesh=mesh,
        in_specs=placed,
        out_specs=(
            P(("groups", "sp", "filt"), None, "in"),
            P("groups", None, "filt", "in"),
            P(("groups", "filt")),
        ),
        check_vma=False,
    )
```

```python
import functools

import jax
import jax.numpy as jnp
from jax import lax
from jax.experimental import pallas as pl
from jax.experimental.pallas import tpu as pltpu
from jax.sharding import PartitionSpec as P

MESH = pl.DeviceIdType.MESH
NT = (((1,), (1,)), ((), ()))


def shift_cols(value, by):
    cols = value.shape[1]
    col = lax.broadcasted_iota(jnp.int32, value.shape, 1)
    if by < 0:
        return jnp.where(col == 0, 0.0, pltpu.roll(value, 1, 1))
    return jnp.where(col == cols - 1, 0.0, pltpu.roll(value, cols - 1, 1))


def lanes(q, cols, count=1):
    return pl.ds(pl.multiple_of(q * cols, cols), count * cols)


def store_shifts(grads, gb_own, place, grad):
    wide = grad.astype(jnp.float32)
    width = gb_own.shape[1]
    gb_own[...] += sum(wide[:, k:k + width] for k in range(0, wide.shape[1], width))
    grads[0, :, place] = shift_cols(wide, 1).astype(jnp.bfloat16)
    grads[2, :, place] = shift_cols(wide, -1).astype(jnp.bfloat16)


def rows_tap(rows, grads, a, start, count):
    cols, depth = rows.shape[1], rows.shape[2]
    o = grads.shape[1]
    window = rows[pl.ds(start + a, count)].reshape(count * cols, depth)
    left = grads[:, :, lanes(start, cols, count)].reshape(3 * o, count * cols)
    return jnp.dot(left, window, preferred_element_type=jnp.float32).reshape(3, o, depth)


def late_row(block, n_f):
    return block * n_f + jnp.where(block > 0, 0, n_f - 1)


def early_row(block, n_f):
    return block * n_f + jnp.where(block > 0, 1, 0)


def gather_kernel(
    n_f, n_s,
    image, weight, bias_in, cotangent,
    rows, grads, gw_own, gb_own, out,
    w, bias, cot, part, peer, act,
    load_sem, ready_z, ready_x, row_send, row_recv, x_send, sum_send, sum_recv,
    g_send, g_recv, h_send, h_recv, out_send, out_recv, cot_send, cot_recv,
):
    p, s, c = lax.axis_index("filt"), lax.axis_index("sp"), lax.axis_index("in")
    sibling = 1 - c
    cols, depth = rows.shape[1], rows.shape[2]
    o = w.shape[2]
    half_c = out.shape[1]
    total = n_f * n_s
    first = s * n_f
    last = n_f - 1
    x_peers = [lax.rem(s + d, n_s) for d in range(1, n_s)]
    pair = n_s == 2
    other = 1 - s
    low = p < n_f // 2
    dist = jnp.where(low, p, last - p)
    early = (low & (s == 0)) | ((p >= n_f // 2) & (s > 0))
    late = (low & (s > 0)) | ((p >= n_f // 2) & (s == 0))
    bound = jnp.where(s == 0, n_f, -1)
    own_bound = jnp.where(s == 0, last, 0)
    bound_at = jnp.maximum(last - dist, jnp.maximum(dist + 1, 2))
    near = n_f // 2

    load_row = pltpu.make_async_copy(image.at[0], rows.at[1 + first + p], load_sem.at[0])
    load_w = pltpu.make_async_copy(
        weight.at[:, :, :, pl.ds(pl.multiple_of(c * depth, depth), depth)], w, load_sem.at[1]
    )
    load_cot = pltpu.make_async_copy(cotangent, cot.at[pl.ds(1, n_f)], load_sem.at[2])
    load_bias = pltpu.make_async_copy(bias_in, bias, load_sem.at[3])
    load_row.start()
    load_w.start()
    load_cot.start()
    load_bias.start()

    barrier = pltpu.get_barrier_semaphore()

    @pl.when(p < last)
    def _():
        pl.semaphore_signal(barrier, 1, device_id={"filt": p + 1}, device_id_type=MESH)

    for peer_s in x_peers:
        @pl.when(peer_s > s)
        def _():
            pl.semaphore_signal(barrier, 1, device_id={"sp": peer_s}, device_id_type=MESH)

    pl.semaphore_signal(barrier, 1, device_id={"in": sibling}, device_id_type=MESH)
    pl.semaphore_wait(barrier, 1 + s + jnp.where(p > 0, 1, 0))

    piece = cols // 2

    def row_copy(q, h, way, where, send):
        slot = rows.at[1 + q, pl.ds(h * piece, piece)]
        return pltpu.make_async_remote_copy(
            src_ref=slot, dst_ref=slot, send_sem=send, recv_sem=row_recv.at[q, h],
            device_id={way: where}, device_id_type=MESH,
        )

    def to_right(q, h):
        return row_copy(q, h, "filt", p + 1, row_send.at[0, q, h])

    def to_left(q, h):
        return row_copy(q, h, "filt", p - 1, row_send.at[1, q, h])

    def to_x(q, h, d):
        return row_copy(first + q, h, "sp", x_peers[d], x_send.at[d, q, h])

    def wait_row(q, h):
        row_copy(q, h, "filt", p, row_send.at[0, 0, 0]).wait_recv()

    def crosses(q, h):
        return ((q > 0) & (q < last)) | (q == p) | (h == 0)

    def pass_on(q, h, right, left):
        if right:
            @pl.when(p < last)
            def _():
                to_right(first + q, h).start()
        if left:
            @pl.when(p > 0)
            def _():
                to_left(first + q, h).start()

        @pl.when(crosses(q, h))
        def _():
            for d in range(n_s - 1):
                to_x(q, h, d).start()

    def own_copy(h, way, where, send):
        place = pl.ds(h * piece, piece)
        return pltpu.make_async_remote_copy(
            src_ref=image.at[0, place], dst_ref=rows.at[1 + first + p, place],
            send_sem=send, recv_sem=row_recv.at[first + p, h],
            device_id={way: where}, device_id_type=MESH,
        )

    def own_to_x(up):
        for d in range(n_s - 1):
            @pl.when((x_peers[d] > s) if up else (x_peers[d] < s))
            def _():
                for h in range(2):
                    own_copy(h, "sp", x_peers[d], x_send.at[d, p, h]).start()

    @pl.when(p > 0)
    def _():
        for h in range(2):
            own_copy(h, "filt", p - 1, row_send.at[1, first + p, h]).start()
        pl.semaphore_signal(ready_z, 1, device_id={"filt": p - 1}, device_id_type=MESH)

    own_to_x(False)
    for peer_s in x_peers:
        @pl.when(peer_s < s)
        def _():
            pl.semaphore_signal(ready_x, 1, device_id={"sp": peer_s}, device_id_type=MESH)

    @pl.when(p < last)
    def _():
        pl.semaphore_wait(ready_z, 1)
        for h in range(2):
            own_copy(h, "filt", p + 1, row_send.at[0, first + p, h]).start()

    @pl.when(s < n_s - 1)
    def _():
        pl.semaphore_wait(ready_x, n_s - 1 - s)

    own_to_x(True)
    load_row.wait()

    zero = jnp.zeros((cols, depth), rows.dtype)
    rows[0] = zero
    rows[total + 1] = zero

    @pl.loop(0, n_f + 2)
    def _(r):
        part[r] = jnp.zeros((o, cols), jnp.float32)

    load_w.wait()

    if pair:
        @pl.loop(0, 9)
        def _(k):
            gw_own[k] = jnp.zeros((o, depth), jnp.float32)

    gb_own[...] = jnp.zeros(gb_own.shape, jnp.float32)

    def add_tap(q, a, r):
        sums = lax.dot_general(
            w[a].reshape(3 * o, depth), rows[1 + q], NT, preferred_element_type=jnp.float32
        )
        part[r + 1] += shift_cols(sums[:o], -1) + sums[o:2 * o] + shift_cols(sums[2 * o:], 1)

    def add_row(q):
        sums = lax.dot_general(
            w[...].reshape(9 * o, depth), rows[1 + first + q], NT, preferred_element_type=jnp.float32
        )
        for a in range(3):
            left, middle, right = (sums[(3 * a + b) * o:(3 * a + b + 1) * o] for b in range(3))
            part[q - a + 2] += shift_cols(left, -1) + middle + shift_cols(right, 1)

    def sum_copy(r):
        return pltpu.make_async_remote_copy(
            src_ref=part.at[r + 1], dst_ref=peer.at[r + 1],
            send_sem=sum_send.at[r + 1], recv_sem=sum_recv.at[r + 1],
            device_id={"in": sibling}, device_id_type=MESH,
        )

    def out_copy(r):
        return pltpu.make_async_remote_copy(
            src_ref=act.at[r, :, pl.ds(pl.multiple_of(c * half_c, half_c), half_c)],
            dst_ref=out.at[pl.ds(pl.multiple_of(p * o, o), o), :],
            send_sem=out_send.at[r], recv_sem=out_recv.at[p],
            device_id={"filt": r}, device_id_type=MESH,
        )

    own_out = pltpu.make_async_copy(
        act.at[p, :, pl.ds(pl.multiple_of(c * half_c, half_c), half_c)],
        out.at[pl.ds(pl.multiple_of(p * o, o), o), :],
        load_sem.at[0],
    )

    half_o = o // 2

    def g_half(q, core):
        return grads.at[1, pl.ds(pl.multiple_of(core * half_o, half_o), half_o), lanes(q, cols)]

    def g_copy(q, d):
        place = g_half(q, c)
        return pltpu.make_async_remote_copy(
            src_ref=place, dst_ref=place, send_sem=g_send.at[d, q], recv_sem=g_recv.at[q],
            device_id={"sp": x_peers[d]}, device_id_type=MESH,
        )

    def h_copy(q, core):
        place = g_half(q, core)
        return pltpu.make_async_remote_copy(
            src_ref=place, dst_ref=place, send_sem=h_send.at[q], recv_sem=h_recv.at[q],
            device_id={"in": sibling}, device_id_type=MESH,
        )

    def half(place, core):
        return place.at[pl.ds(pl.multiple_of(core * half_o, half_o), half_o)]

    def cot_copy():
        return pltpu.make_async_remote_copy(
            src_ref=half(cotangent.at[own_bound], c),
            dst_ref=half(cot.at[jnp.where(s == 0, 0, n_f + 1)], c),
            send_sem=cot_send.at[0], recv_sem=cot_recv.at[0],
            device_id={"sp": other}, device_id_type=MESH,
        )

    def cot_share(core):
        place = half(cot.at[bound + 1], core)
        return pltpu.make_async_remote_copy(
            src_ref=place, dst_ref=place, send_sem=cot_send.at[1], recv_sem=cot_recv.at[1],
            device_id={"in": sibling}, device_id_type=MESH,
        )

    def done_at(r):
        low = jnp.where(s == 0, jnp.maximum(p, 1), jnp.maximum(p, n_f - p))
        high = jnp.where(
            s == n_s - 1, jnp.maximum(last - p, 1), jnp.maximum(last - p, p + 1)
        )
        return jnp.where(r == 0, low, jnp.where(r == last, high, jnp.abs(r - p) + 1))

    def finished_at(r):
        if not pair:
            return done_at(r)
        return jnp.where(
            (dist > 0) & (done_at(r) < last - dist), done_at(r) + 1, done_at(r)
        )

    def sends_grad(r):
        return early | (r != own_bound) if pair else r >= 0

    def activate(r):
        sum_copy(r).wait_recv()
        bias_all = jnp.broadcast_to(bias[...], (cols, o)).T
        shifted = part[r + 1] + peer[r + 1] + bias_all
        sig = jax.nn.sigmoid(shifted)
        slope = sig * (1.0 + shifted * (1.0 - sig))
        grad = (cot[r + 1].astype(jnp.float32) * slope).astype(jnp.bfloat16)
        grads[1, :, lanes(first + r, cols)] = grad
        return grad, (shifted * sig).astype(jnp.bfloat16)

    def finish(r):
        grad, value = activate(r)
        act[r] = value

        @pl.when(sends_grad(r))
        def _():
            for d in range(n_s - 1):
                g_copy(first + r, d).start()

        send_out(r)
        store_shifts(grads, gb_own, lanes(first + r, cols), grad)

    def finish_bound():
        grad, _ = activate(bound)
        store_shifts(grads, gb_own, lanes(first + bound, cols), grad)

    def send_out(r):
        @pl.when(r == p)
        def _():
            own_out.start()

        @pl.when(r != p)
        def _():
            out_copy(r).start()

    add_row(p)
    load_cot.wait()
    load_bias.wait()

    def relay(t):
        @pl.when(t == p + 1)
        def _():
            for block in x_peers:
                wait_row(block * n_f, 1)

                @pl.when(p < last)
                def _():
                    to_right(block * n_f, 1).start()

        @pl.when(t == n_f - p)
        def _():
            for block in x_peers:
                wait_row(block * n_f + last, 1)

                @pl.when(p > 0)
                def _():
                    to_left(block * n_f + last, 1).start()

    def settle(t):
        @pl.when(t == p + 1)
        def _():
            for block in x_peers:
                wait_row(block * n_f, 0)

        @pl.when(t == n_f - p)
        def _():
            for block in x_peers:
                wait_row(block * n_f + last, 0)

    def add_edges(t):
        if pair:
            tap = jnp.where(s == 0, 2, 0)
            edge = jnp.where(s == 0, first + n_f, first - 1)
            after = jnp.where(s == 0, first + n_f + 1, first - 2)

            @pl.when(t == jnp.where(early, dist + 1, n_f - dist))
            def _():
                add_tap(edge, tap, own_bound)

            @pl.when(early & (t == dist + 1))
            def _():
                add_tap(edge, 1, bound)

            @pl.when(early & (t == jnp.maximum(dist + 1, 2)))
            def _():
                for h in range(2):
                    wait_row(after, h)
                add_tap(after, tap, bound)

            return

        @pl.when((t == p + 1) & (s < n_s - 1))
        def _():
            add_tap(first + n_f, 2, last)

        @pl.when((t == n_f - p) & (s > 0))
        def _():
            add_tap(first - 1, 0, 0)

    def start_sums(t):
        @pl.loop(0, n_f)
        def _(r):
            @pl.when(done_at(r) == t)
            def _():
                sum_copy(r).start()

        if pair:
            @pl.when(early & (t == bound_at))
            def _():
                sum_copy(bound).start()

    def finish_rows(t):
        @pl.loop(0, n_f)
        def _(r):
            @pl.when(finished_at(r) == t)
            def _():
                finish(r)

    own_start = early_row(s, n_f)

    def own_rows(a):
        gw_own[3 * a:3 * a + 3] = rows_tap(rows, grads, a, own_start, n_f - 1)

    def add_rows(a, start, count):
        gw_own[3 * a:3 * a + 3] += rows_tap(rows, grads, a, start, count)

    def share_grad(q):
        g_copy(q, 0).wait_recv()
        h_copy(q, c).start()

    def take_grad(q):
        h_copy(q, sibling).wait_recv()
        place = lanes(q, cols)
        store_shifts(grads, gb_own, place, grads[1, :, place])

    def add_all(start, count):
        for a in range(3):
            add_rows(a, start, count)

    def near_rows():
        @pl.when(early)
        def _():
            add_all(first + jnp.where(low, 0, n_f - near), near)

        @pl.when(late)
        def _():
            add_all(first + jnp.where(low, 1, n_f - near), near - 1)

    def far_rows():
        add_all(first + jnp.where(low, near, 0), n_f - near)

    def tail_of_pair():
        def place(k):
            return other * n_f + jnp.where(low, k, last - k)

        @pl.when(early)
        def _():
            cot_copy().wait_recv()
            cot_share(c).start()

        @pl.when(late)
        def _():
            share_grad(place(0))

        @pl.when(dist == 0)
        def _():
            far_rows()

        @pl.loop(1, near)
        def _(k):
            share_grad(place(k))

        @pl.when(early)
        def _():
            cot_share(sibling).wait_recv()
            finish_bound()

        relay(n_f)
        settle(n_f)

        @pl.when(late)
        def _():
            add_edges(n_f)
            start_sums(n_f)
            take_grad(place(0))
            for h in range(2):
                wait_row(place(1), h)

        @pl.loop(1, near)
        def _(k):
            take_grad(place(k))

        @pl.loop(2, last)
        def _(k):
            for h in range(2):
                wait_row(place(k), h)

        add_all(other * n_f + jnp.where(low, 0, n_f - near), near)

        @pl.when(late)
        def _():
            finish_rows(n_f)
            add_all(first + own_bound, 1)

        @pl.loop(near, n_f)
        def _(k):
            share_grad(place(k))

        @pl.loop(near, n_f)
        def _(k):
            take_grad(place(k))

    def tail_of_many():
        relay(n_f)
        settle(n_f)
        add_edges(n_f)
        start_sums(n_f)
        finish_rows(n_f)
        for a in range(3):
            own_rows(a)

        for block in x_peers:
            start = early_row(block, n_f)

            @pl.loop(1, last)
            def _(q):
                for h in range(2):
                    wait_row(block * n_f + q, h)

            @pl.loop(0, n_f - 1)
            def _(q):
                share_grad(start + q)

            @pl.loop(0, n_f - 1)
            def _(q):
                take_grad(start + q)

            for a in range(3):
                add_rows(a, start, n_f - 1)


        for block in x_peers:
            share_grad(late_row(block, n_f))
            take_grad(late_row(block, n_f))

    @pl.loop(1, n_f)
    def _(t):
        for h in range(2):
            @pl.when(p - t >= 0)
            def _():
                wait_row(first + p - t, h)
                pass_on(p - t, h, True, False)

            @pl.when(p + t < n_f)
            def _():
                wait_row(first + p + t, h)
                pass_on(p + t, h, False, True)

        relay(t)

        if pair:
            @pl.when((t == last) & (dist > 0))
            def _():
                near_rows()
                far_rows()

        settle(t)

        @pl.when(p - t >= 0)
        def _():
            add_row(p - t)

        @pl.when(p + t < n_f)
        def _():
            add_row(p + t)

        add_edges(t)
        start_sums(t)

        if pair:
            @pl.when(late & (t == n_f - 2))
            def _():
                cot_copy().start()

        finish_rows(t)

        if pair:
            @pl.when((t == n_f - 2) & (dist == 0))
            def _():
                near_rows()

    if pair:
        tail_of_pair()
    else:
        tail_of_many()

    @pl.loop(0, n_f)
    def _(r):
        sum_copy(r).wait_send()

        @pl.when(r == p)
        def _():
            own_out.wait()

        @pl.when(r != p)
        def _():
            out_copy(r).wait_send()
            pltpu.make_async_remote_copy(
                src_ref=act.at[r, :, pl.ds(0, half_c)],
                dst_ref=out.at[pl.ds(pl.multiple_of(r * o, o), o), :],
                send_sem=out_send.at[r], recv_sem=out_recv.at[r],
                device_id={"filt": r}, device_id_type=MESH,
            ).wait_recv()

        for d in range(n_s - 1):
            @pl.when(sends_grad(r))
            def _():
                g_copy(first + r, d).wait_send()

            for h in range(2):
                @pl.when(crosses(r, h))
                def _():
                    to_x(r, h, d).wait_send()

        @pl.when((r <= p) & (p < last))
        def _():
            for h in range(2):
                to_right(first + r, h).wait_send()

        @pl.when((r >= p) & (p > 0))
        def _():
            for h in range(2):
                to_left(first + r, h).wait_send()

    for block in x_peers:
        @pl.loop(0, n_f)
        def _(q):
            if pair:
                @pl.when(late | (q != jnp.where(low, 0, last)))
                def _():
                    h_copy(block * n_f + q, c).wait_send()
            else:
                h_copy(block * n_f + q, c).wait_send()

        @pl.when(p < last)
        def _():
            to_right(block * n_f, 1).wait_send()

        @pl.when(p > 0)
        def _():
            to_left(block * n_f + last, 1).wait_send()

    if pair:
        @pl.when(early)
        def _():
            sum_copy(bound).wait_send()
            cot_share(c).wait_send()

        @pl.when(late)
        def _():
            cot_copy().wait_send()


def finish_kernel(n_f, n_s, rows, grads, gw_own, gb_own, out_in, gw, gb, out, total, sem, out_sem):
    cols = rows.shape[1]
    out_copy = pltpu.make_async_copy(out_in, out.at[0], out_sem)
    out_copy.start()

    if n_s == 2:
        p, s = lax.axis_index("filt"), lax.axis_index("sp")
        late = [((1 - s) * n_f + jnp.where(p < n_f // 2, n_f // 2, 0), n_f - n_f // 2)]
    else:
        late = [(n_f - 1, 2)] + [(block * n_f, 1) for block in range(2, n_s)]

    def gw_copy(k):
        return pltpu.make_async_copy(total.at[k], gw.at[k // 3, k % 3], sem.at[k])

    gb[...] = jnp.sum(gb_own[...].T, axis=0, keepdims=True)

    for a in range(3):
        value = gw_own[3 * a:3 * a + 3]
        for start, count in late:
            value = value + rows_tap(rows, grads, a, start, count)
        for b in range(3):
            total[3 * a + b] = value[b]
            gw_copy(3 * a + b).start()

    for k in range(9):
        gw_copy(k).wait()

    out_copy.wait()


def on_device(image, weight, bias, cotangent):
    n_f, n_s, n_in = (lax.axis_size(name) for name in ("filt", "sp", "in"))
    row_count, o, cols = cotangent.shape
    depth = image.shape[2]
    total = n_f * n_s
    any_space = pl.BlockSpec(memory_space=pl.ANY)
    vmem = pl.BlockSpec(memory_space=pltpu.VMEM)
    hbm = pl.BlockSpec(memory_space=pltpu.HBM)
    dma = pltpu.SemaphoreType.DMA
    between = pl.pallas_call(
        functools.partial(gather_kernel, n_f, n_s),
        out_shape=(
            pltpu.VMEM((total + 2, cols, depth), jnp.bfloat16),
            pltpu.VMEM((3, o, total * cols), jnp.bfloat16),
            pltpu.VMEM((9, o, depth), jnp.float32),
            pltpu.VMEM((o, 128), jnp.float32),
            pltpu.VMEM((n_f * o, cols // n_in), jnp.bfloat16),
        ),
        in_specs=[hbm, hbm, hbm, hbm],
        out_specs=(vmem,) * 5,
        scratch_shapes=[
            pltpu.VMEM((3, 3, o, depth), jnp.bfloat16),
            pltpu.VMEM((1, o), jnp.float32),
            pltpu.VMEM((n_f + 2, o, cols), jnp.bfloat16),
            pltpu.VMEM((n_f + 2, o, cols), jnp.float32),
            pltpu.VMEM((n_f + 2, o, cols), jnp.float32),
            pltpu.VMEM((n_f, o, cols), jnp.bfloat16),
            dma((4,)),
            pltpu.SemaphoreType.REGULAR,
            pltpu.SemaphoreType.REGULAR,
            dma((2, total, 2)),
            dma((total, 2)),
            dma((n_s - 1, n_f, 2)),
            dma((n_f + 2,)),
            dma((n_f + 2,)),
            dma((n_s - 1, total)),
            dma((total,)),
            dma((total,)),
            dma((total,)),
            dma((n_f,)),
            dma((n_f,)),
            dma((2,)),
            dma((2,)),
        ],
        compiler_params=pltpu.CompilerParams(
            collective_id=0, has_side_effects=True, vmem_limit_bytes=24 * 1024 * 1024
        ),
        name="gather",
    )(*(
        pltpu.with_memory_space_constraint(x, pltpu.HBM)
        for x in (image, weight, bias.reshape(1, o), cotangent)
    ))
    grad_weight, grad_bias, output = pl.pallas_call(
        functools.partial(finish_kernel, n_f, n_s),
        out_shape=(
            jax.ShapeDtypeStruct((3, 3, o, depth), jnp.float32),
            jax.ShapeDtypeStruct((1, o), jnp.float32),
            jax.ShapeDtypeStruct((1, n_f * o, cols // n_in), jnp.bfloat16),
        ),
        in_specs=[vmem] * 5,
        out_specs=(any_space, vmem, any_space),
        scratch_shapes=[
            pltpu.VMEM((9, o, depth), jnp.float32),
            dma((9,)),
            dma(()),
        ],
        compiler_params=pltpu.CompilerParams(vmem_limit_bytes=20 * 1024 * 1024),
        name="finish",
    )(*between)
    return (output, grad_weight, grad_bias.reshape(o))


def solution(mesh):
    placed = (
        P(("groups", "sp", "filt"), None, "in"),
        P(None, None, "filt", None),
        P("filt"),
        P(("groups", "sp"), "filt", None),
    )
    return jax.shard_map(
        on_device,
        mesh=mesh,
        in_specs=placed,
        out_specs=(
            P(("groups", "sp", "filt"), None, "in"),
            P("groups", None, "filt", "in"),
            P(("groups", "filt")),
        ),
        check_vma=False,
    )
```

```python
import functools

import jax
import jax.numpy as jnp
from jax import lax
from jax.experimental import pallas as pl
from jax.experimental.pallas import tpu as pltpu
from jax.sharding import PartitionSpec as P

MESH = pl.DeviceIdType.MESH
NT = (((1,), (1,)), ((), ()))


def shift_cols(value, by):
    cols = value.shape[1]
    col = lax.broadcasted_iota(jnp.int32, value.shape, 1)
    if by < 0:
        return jnp.where(col == 0, 0.0, pltpu.roll(value, 1, 1))
    return jnp.where(col == cols - 1, 0.0, pltpu.roll(value, cols - 1, 1))


def lanes(q, cols, count=1):
    return pl.ds(pl.multiple_of(q * cols, cols), count * cols)


def store_shifts(grads, gb_own, place, grad):
    wide = grad.astype(jnp.float32)
    width = gb_own.shape[1]
    gb_own[...] += sum(wide[:, k:k + width] for k in range(0, wide.shape[1], width))
    grads[0, :, place] = shift_cols(wide, 1).astype(jnp.bfloat16)
    grads[2, :, place] = shift_cols(wide, -1).astype(jnp.bfloat16)


def rows_tap(rows, grads, a, start, count):
    cols, depth = rows.shape[1], rows.shape[2]
    o = grads.shape[1]
    window = rows[pl.ds(start + a, count)].reshape(count * cols, depth)
    left = grads[:, :, lanes(start, cols, count)].reshape(3 * o, count * cols)
    return jnp.dot(left, window, preferred_element_type=jnp.float32).reshape(3, o, depth)


def late_row(block, n_f):
    return block * n_f + jnp.where(block > 0, 0, n_f - 1)


def early_row(block, n_f):
    return block * n_f + jnp.where(block > 0, 1, 0)


def gather_kernel(
    n_f, n_s,
    image, weight, bias_in, cotangent,
    rows, grads, gw_own, gb_own, out,
    w, bias, cot, part, peer, act,
    load_sem, ready_z, ready_x, row_send, row_recv, x_send, sum_send, sum_recv,
    g_send, g_recv, h_send, h_recv, out_send, out_recv, cot_send, cot_recv,
):
    p, s, c = lax.axis_index("filt"), lax.axis_index("sp"), lax.axis_index("in")
    sibling = 1 - c
    cols, depth = rows.shape[1], rows.shape[2]
    o = w.shape[2]
    half_c = out.shape[1]
    total = n_f * n_s
    first = s * n_f
    last = n_f - 1
    x_peers = [lax.rem(s + d, n_s) for d in range(1, n_s)]
    pair = n_s == 2
    other = 1 - s
    low = p < n_f // 2
    dist = jnp.where(low, p, last - p)
    early = (low & (s == 0)) | ((p >= n_f // 2) & (s > 0))
    late = (low & (s > 0)) | ((p >= n_f // 2) & (s == 0))
    bound = jnp.where(s == 0, n_f, -1)
    own_bound = jnp.where(s == 0, last, 0)
    bound_at = jnp.maximum(last - dist, jnp.maximum(dist + 1, 2))
    near = n_f // 2

    load_row = pltpu.make_async_copy(image.at[0], rows.at[1 + first + p], load_sem.at[0])
    load_w = pltpu.make_async_copy(
        weight.at[:, :, :, pl.ds(pl.multiple_of(c * depth, depth), depth)], w, load_sem.at[1]
    )
    load_cot = pltpu.make_async_copy(cotangent, cot.at[pl.ds(1, n_f)], load_sem.at[2])
    load_bias = pltpu.make_async_copy(bias_in, bias, load_sem.at[3])
    barrier = pltpu.get_barrier_semaphore()

    @pl.when(p < last)
    def _():
        pl.semaphore_signal(barrier, 1, device_id={"filt": p + 1}, device_id_type=MESH)

    for peer_s in x_peers:
        @pl.when(peer_s > s)
        def _():
            pl.semaphore_signal(barrier, 1, device_id={"sp": peer_s}, device_id_type=MESH)

    pl.semaphore_signal(barrier, 1, device_id={"in": sibling}, device_id_type=MESH)
    pl.semaphore_wait(barrier, 1 + s + jnp.where(p > 0, 1, 0))

    cut = cols * 7 // 16

    def span(h):
        return pl.ds(0, cut) if h == 0 else pl.ds(cut, cols - cut)

    def row_copy(q, h, way, where, send):
        slot = rows.at[1 + q, span(h)]
        return pltpu.make_async_remote_copy(
            src_ref=slot, dst_ref=slot, send_sem=send, recv_sem=row_recv.at[q, h],
            device_id={way: where}, device_id_type=MESH,
        )

    def to_right(q, h):
        return row_copy(q, h, "filt", p + 1, row_send.at[0, q, h])

    def to_left(q, h):
        return row_copy(q, h, "filt", p - 1, row_send.at[1, q, h])

    def to_x(q, h, d):
        return row_copy(first + q, h, "sp", x_peers[d], x_send.at[d, q, h])

    def wait_row(q, h):
        row_copy(q, h, "filt", p, row_send.at[0, 0, 0]).wait_recv()

    def crosses(q, h):
        return ((q > 0) & (q < last)) | (q == p) | (h == 0)

    def pass_on(q, h, right, left):
        if right:
            @pl.when(p < last)
            def _():
                to_right(first + q, h).start()
        if left:
            @pl.when(p > 0)
            def _():
                to_left(first + q, h).start()

        @pl.when(crosses(q, h))
        def _():
            for d in range(n_s - 1):
                to_x(q, h, d).start()

    def own_copy(h, way, where, send):
        place = span(h)
        return pltpu.make_async_remote_copy(
            src_ref=image.at[0, place], dst_ref=rows.at[1 + first + p, place],
            send_sem=send, recv_sem=row_recv.at[first + p, h],
            device_id={way: where}, device_id_type=MESH,
        )

    def own_to_x(up):
        for d in range(n_s - 1):
            @pl.when((x_peers[d] > s) if up else (x_peers[d] < s))
            def _():
                for h in range(2):
                    own_copy(h, "sp", x_peers[d], x_send.at[d, p, h]).start()

    @pl.when(p > 0)
    def _():
        for h in range(2):
            own_copy(h, "filt", p - 1, row_send.at[1, first + p, h]).start()
        pl.semaphore_signal(ready_z, 1, device_id={"filt": p - 1}, device_id_type=MESH)

    own_to_x(False)
    for peer_s in x_peers:
        @pl.when(peer_s < s)
        def _():
            pl.semaphore_signal(ready_x, 1, device_id={"sp": peer_s}, device_id_type=MESH)

    load_row.start()
    load_w.start()
    load_cot.start()
    load_bias.start()

    @pl.when(p < last)
    def _():
        pl.semaphore_wait(ready_z, 1)
        for h in range(2):
            own_copy(h, "filt", p + 1, row_send.at[0, first + p, h]).start()

    @pl.when(s < n_s - 1)
    def _():
        pl.semaphore_wait(ready_x, n_s - 1 - s)

    own_to_x(True)
    load_row.wait()

    zero = jnp.zeros((cols, depth), rows.dtype)
    rows[0] = zero
    rows[total + 1] = zero

    @pl.loop(0, n_f + 2)
    def _(r):
        part[r] = jnp.zeros((o, cols), jnp.float32)

    load_w.wait()

    if pair:
        @pl.loop(0, 9)
        def _(k):
            gw_own[k] = jnp.zeros((o, depth), jnp.float32)

    gb_own[...] = jnp.zeros(gb_own.shape, jnp.float32)

    def add_tap(q, a, r):
        sums = lax.dot_general(
            w[a].reshape(3 * o, depth), rows[1 + q], NT, preferred_element_type=jnp.float32
        )
        part[r + 1] += shift_cols(sums[:o], -1) + sums[o:2 * o] + shift_cols(sums[2 * o:], 1)

    def add_row(q):
        sums = lax.dot_general(
            w[...].reshape(9 * o, depth), rows[1 + first + q], NT, preferred_element_type=jnp.float32
        )
        for a in range(3):
            left, middle, right = (sums[(3 * a + b) * o:(3 * a + b + 1) * o] for b in range(3))
            part[q - a + 2] += shift_cols(left, -1) + middle + shift_cols(right, 1)

    def sum_copy(r):
        return pltpu.make_async_remote_copy(
            src_ref=part.at[r + 1], dst_ref=peer.at[r + 1],
            send_sem=sum_send.at[r + 1], recv_sem=sum_recv.at[r + 1],
            device_id={"in": sibling}, device_id_type=MESH,
        )

    def out_copy(r):
        return pltpu.make_async_remote_copy(
            src_ref=act.at[r, :, pl.ds(pl.multiple_of(c * half_c, half_c), half_c)],
            dst_ref=out.at[pl.ds(pl.multiple_of(p * o, o), o), :],
            send_sem=out_send.at[r], recv_sem=out_recv.at[p],
            device_id={"filt": r}, device_id_type=MESH,
        )

    own_out = pltpu.make_async_copy(
        act.at[p, :, pl.ds(pl.multiple_of(c * half_c, half_c), half_c)],
        out.at[pl.ds(pl.multiple_of(p * o, o), o), :],
        load_sem.at[0],
    )

    half_o = o // 2

    def g_half(q, core):
        return grads.at[1, pl.ds(pl.multiple_of(core * half_o, half_o), half_o), lanes(q, cols)]

    def g_copy(q, d):
        place = g_half(q, c)
        return pltpu.make_async_remote_copy(
            src_ref=place, dst_ref=place, send_sem=g_send.at[d, q], recv_sem=g_recv.at[q],
            device_id={"sp": x_peers[d]}, device_id_type=MESH,
        )

    def h_copy(q, core):
        place = g_half(q, core)
        return pltpu.make_async_remote_copy(
            src_ref=place, dst_ref=place, send_sem=h_send.at[q], recv_sem=h_recv.at[q],
            device_id={"in": sibling}, device_id_type=MESH,
        )

    def half(place, core):
        return place.at[pl.ds(pl.multiple_of(core * half_o, half_o), half_o)]

    def cot_copy():
        return pltpu.make_async_remote_copy(
            src_ref=half(cotangent.at[own_bound], c),
            dst_ref=half(cot.at[jnp.where(s == 0, 0, n_f + 1)], c),
            send_sem=cot_send.at[0], recv_sem=cot_recv.at[0],
            device_id={"sp": other}, device_id_type=MESH,
        )

    def cot_share(core):
        place = half(cot.at[bound + 1], core)
        return pltpu.make_async_remote_copy(
            src_ref=place, dst_ref=place, send_sem=cot_send.at[1], recv_sem=cot_recv.at[1],
            device_id={"in": sibling}, device_id_type=MESH,
        )

    def done_at(r):
        low = jnp.where(s == 0, jnp.maximum(p, 1), jnp.maximum(p, n_f - p))
        high = jnp.where(
            s == n_s - 1, jnp.maximum(last - p, 1), jnp.maximum(last - p, p + 1)
        )
        return jnp.where(r == 0, low, jnp.where(r == last, high, jnp.abs(r - p) + 1))

    def finished_at(r):
        if not pair:
            return done_at(r)
        return jnp.where(
            (dist > 0) & (done_at(r) < last - dist), done_at(r) + 1, done_at(r)
        )

    def sends_grad(r):
        return early | (r != own_bound) if pair else r >= 0

    def activate(r):
        sum_copy(r).wait_recv()
        bias_all = jnp.broadcast_to(bias[...], (cols, o)).T
        shifted = part[r + 1] + peer[r + 1] + bias_all
        sig = jax.nn.sigmoid(shifted)
        slope = sig * (1.0 + shifted * (1.0 - sig))
        grad = (cot[r + 1].astype(jnp.float32) * slope).astype(jnp.bfloat16)
        grads[1, :, lanes(first + r, cols)] = grad
        return grad, (shifted * sig).astype(jnp.bfloat16)

    def finish(r):
        grad, value = activate(r)
        act[r] = value

        @pl.when(sends_grad(r))
        def _():
            for d in range(n_s - 1):
                g_copy(first + r, d).start()

        send_out(r)
        store_shifts(grads, gb_own, lanes(first + r, cols), grad)

    def finish_bound():
        grad, _ = activate(bound)
        store_shifts(grads, gb_own, lanes(first + bound, cols), grad)

    def send_out(r):
        @pl.when(r == p)
        def _():
            own_out.start()

        @pl.when(r != p)
        def _():
            out_copy(r).start()

    add_row(p)
    load_cot.wait()
    load_bias.wait()

    def relay(t):
        @pl.when(t == p + 1)
        def _():
            for block in x_peers:
                wait_row(block * n_f, 1)

                @pl.when(p < last)
                def _():
                    to_right(block * n_f, 1).start()

        @pl.when(t == n_f - p)
        def _():
            for block in x_peers:
                wait_row(block * n_f + last, 1)

                @pl.when(p > 0)
                def _():
                    to_left(block * n_f + last, 1).start()

    def settle(t):
        @pl.when(t == p + 1)
        def _():
            for block in x_peers:
                wait_row(block * n_f, 0)

        @pl.when(t == n_f - p)
        def _():
            for block in x_peers:
                wait_row(block * n_f + last, 0)

    def add_edges(t):
        if pair:
            tap = jnp.where(s == 0, 2, 0)
            edge = jnp.where(s == 0, first + n_f, first - 1)
            after = jnp.where(s == 0, first + n_f + 1, first - 2)

            @pl.when(t == jnp.where(early, dist + 1, n_f - dist))
            def _():
                add_tap(edge, tap, own_bound)

            @pl.when(early & (t == dist + 1))
            def _():
                add_tap(edge, 1, bound)

            @pl.when(early & (t == jnp.maximum(dist + 1, 2)))
            def _():
                for h in range(2):
                    wait_row(after, h)
                add_tap(after, tap, bound)

            return

        @pl.when((t == p + 1) & (s < n_s - 1))
        def _():
            add_tap(first + n_f, 2, last)

        @pl.when((t == n_f - p) & (s > 0))
        def _():
            add_tap(first - 1, 0, 0)

    def start_sums(t):
        @pl.loop(0, n_f)
        def _(r):
            @pl.when(done_at(r) == t)
            def _():
                sum_copy(r).start()

        if pair:
            @pl.when(early & (t == bound_at))
            def _():
                sum_copy(bound).start()

    def finish_rows(t):
        @pl.loop(0, n_f)
        def _(r):
            @pl.when(finished_at(r) == t)
            def _():
                finish(r)

    own_start = early_row(s, n_f)

    def own_rows(a):
        gw_own[3 * a:3 * a + 3] = rows_tap(rows, grads, a, own_start, n_f - 1)

    def add_rows(a, start, count):
        gw_own[3 * a:3 * a + 3] += rows_tap(rows, grads, a, start, count)

    def share_grad(q):
        g_copy(q, 0).wait_recv()
        h_copy(q, c).start()

    def take_grad(q):
        h_copy(q, sibling).wait_recv()
        place = lanes(q, cols)
        store_shifts(grads, gb_own, place, grads[1, :, place])

    def add_all(start, count):
        for a in range(3):
            add_rows(a, start, count)

    def near_rows():
        @pl.when(early)
        def _():
            add_all(first + jnp.where(low, 0, n_f - near), near)

        @pl.when(late)
        def _():
            add_all(first + jnp.where(low, 1, n_f - near), near - 1)

    def far_rows():
        add_all(first + jnp.where(low, near, 0), n_f - near)

    def tail_of_pair():
        def place(k):
            return other * n_f + jnp.where(low, k, last - k)

        @pl.when(early)
        def _():
            cot_copy().wait_recv()
            cot_share(c).start()

        @pl.when(late)
        def _():
            share_grad(place(0))

        @pl.when(dist == 0)
        def _():
            far_rows()

        @pl.loop(1, near)
        def _(k):
            share_grad(place(k))

        @pl.when(early)
        def _():
            cot_share(sibling).wait_recv()
            finish_bound()

        relay(n_f)
        settle(n_f)

        @pl.when(late)
        def _():
            add_edges(n_f)
            start_sums(n_f)
            take_grad(place(0))
            for h in range(2):
                wait_row(place(1), h)

        @pl.loop(1, near)
        def _(k):
            take_grad(place(k))

        @pl.loop(2, last)
        def _(k):
            for h in range(2):
                wait_row(place(k), h)

        add_all(other * n_f + jnp.where(low, 0, n_f - near), near)

        @pl.when(late)
        def _():
            finish_rows(n_f)
            add_all(first + own_bound, 1)

        @pl.loop(near, n_f)
        def _(k):
            share_grad(place(k))

        @pl.loop(near, n_f)
        def _(k):
            take_grad(place(k))

    def tail_of_many():
        relay(n_f)
        settle(n_f)
        add_edges(n_f)
        start_sums(n_f)
        finish_rows(n_f)
        for a in range(3):
            own_rows(a)

        for block in x_peers:
            start = early_row(block, n_f)

            @pl.loop(1, last)
            def _(q):
                for h in range(2):
                    wait_row(block * n_f + q, h)

            @pl.loop(0, n_f - 1)
            def _(q):
                share_grad(start + q)

            @pl.loop(0, n_f - 1)
            def _(q):
                take_grad(start + q)

            for a in range(3):
                add_rows(a, start, n_f - 1)


        for block in x_peers:
            share_grad(late_row(block, n_f))
            take_grad(late_row(block, n_f))

    @pl.loop(1, n_f)
    def _(t):
        for h in range(2):
            @pl.when(p - t >= 0)
            def _():
                wait_row(first + p - t, h)
                pass_on(p - t, h, True, False)

            @pl.when(p + t < n_f)
            def _():
                wait_row(first + p + t, h)
                pass_on(p + t, h, False, True)

        relay(t)

        if pair:
            @pl.when((t == last) & (dist > 0))
            def _():
                near_rows()
                far_rows()

        settle(t)

        @pl.when(p - t >= 0)
        def _():
            add_row(p - t)

        @pl.when(p + t < n_f)
        def _():
            add_row(p + t)

        add_edges(t)
        start_sums(t)

        if pair:
            @pl.when(late & (t == n_f - 2))
            def _():
                cot_copy().start()

        finish_rows(t)

        if pair:
            @pl.when((t == n_f - 2) & (dist == 0))
            def _():
                near_rows()

    if pair:
        tail_of_pair()
    else:
        tail_of_many()

    @pl.loop(0, n_f)
    def _(r):
        sum_copy(r).wait_send()

        @pl.when(r == p)
        def _():
            own_out.wait()

        @pl.when(r != p)
        def _():
            out_copy(r).wait_send()
            pltpu.make_async_remote_copy(
                src_ref=act.at[r, :, pl.ds(0, half_c)],
                dst_ref=out.at[pl.ds(pl.multiple_of(r * o, o), o), :],
                send_sem=out_send.at[r], recv_sem=out_recv.at[r],
                device_id={"filt": r}, device_id_type=MESH,
            ).wait_recv()

        for d in range(n_s - 1):
            @pl.when(sends_grad(r))
            def _():
                g_copy(first + r, d).wait_send()

            for h in range(2):
                @pl.when(crosses(r, h))
                def _():
                    to_x(r, h, d).wait_send()

        @pl.when((r <= p) & (p < last))
        def _():
            for h in range(2):
                to_right(first + r, h).wait_send()

        @pl.when((r >= p) & (p > 0))
        def _():
            for h in range(2):
                to_left(first + r, h).wait_send()

    for block in x_peers:
        @pl.loop(0, n_f)
        def _(q):
            if pair:
                @pl.when(late | (q != jnp.where(low, 0, last)))
                def _():
                    h_copy(block * n_f + q, c).wait_send()
            else:
                h_copy(block * n_f + q, c).wait_send()

        @pl.when(p < last)
        def _():
            to_right(block * n_f, 1).wait_send()

        @pl.when(p > 0)
        def _():
            to_left(block * n_f + last, 1).wait_send()

    if pair:
        @pl.when(early)
        def _():
            sum_copy(bound).wait_send()
            cot_share(c).wait_send()

        @pl.when(late)
        def _():
            cot_copy().wait_send()


def finish_kernel(n_f, n_s, rows, grads, gw_own, gb_own, out_in, gw, gb, out, total, sem, out_sem):
    cols = rows.shape[1]
    out_copy = pltpu.make_async_copy(out_in, out.at[0], out_sem)
    out_copy.start()

    if n_s == 2:
        p, s = lax.axis_index("filt"), lax.axis_index("sp")
        late = [((1 - s) * n_f + jnp.where(p < n_f // 2, n_f // 2, 0), n_f - n_f // 2)]
    else:
        late = [(n_f - 1, 2)] + [(block * n_f, 1) for block in range(2, n_s)]

    def gw_copy(k):
        return pltpu.make_async_copy(total.at[k], gw.at[k // 3, k % 3], sem.at[k])

    gb[...] = jnp.sum(gb_own[...].T, axis=0, keepdims=True)

    for a in range(3):
        value = gw_own[3 * a:3 * a + 3]
        for start, count in late:
            value = value + rows_tap(rows, grads, a, start, count)
        for b in range(3):
            total[3 * a + b] = value[b]
            gw_copy(3 * a + b).start()

    for k in range(9):
        gw_copy(k).wait()

    out_copy.wait()


def on_device(image, weight, bias, cotangent):
    n_f, n_s, n_in = (lax.axis_size(name) for name in ("filt", "sp", "in"))
    row_count, o, cols = cotangent.shape
    depth = image.shape[2]
    total = n_f * n_s
    any_space = pl.BlockSpec(memory_space=pl.ANY)
    vmem = pl.BlockSpec(memory_space=pltpu.VMEM)
    hbm = pl.BlockSpec(memory_space=pltpu.HBM)
    dma = pltpu.SemaphoreType.DMA
    between = pl.pallas_call(
        functools.partial(gather_kernel, n_f, n_s),
        out_shape=(
            pltpu.VMEM((total + 2, cols, depth), jnp.bfloat16),
            pltpu.VMEM((3, o, total * cols), jnp.bfloat16),
            pltpu.VMEM((9, o, depth), jnp.float32),
            pltpu.VMEM((o, 128), jnp.float32),
            pltpu.VMEM((n_f * o, cols // n_in), jnp.bfloat16),
        ),
        in_specs=[hbm, hbm, hbm, hbm],
        out_specs=(vmem,) * 5,
        scratch_shapes=[
            pltpu.VMEM((3, 3, o, depth), jnp.bfloat16),
            pltpu.VMEM((1, o), jnp.float32),
            pltpu.VMEM((n_f + 2, o, cols), jnp.bfloat16),
            pltpu.VMEM((n_f + 2, o, cols), jnp.float32),
            pltpu.VMEM((n_f + 2, o, cols), jnp.float32),
            pltpu.VMEM((n_f, o, cols), jnp.bfloat16),
            dma((4,)),
            pltpu.SemaphoreType.REGULAR,
            pltpu.SemaphoreType.REGULAR,
            dma((2, total, 2)),
            dma((total, 2)),
            dma((n_s - 1, n_f, 2)),
            dma((n_f + 2,)),
            dma((n_f + 2,)),
            dma((n_s - 1, total)),
            dma((total,)),
            dma((total,)),
            dma((total,)),
            dma((n_f,)),
            dma((n_f,)),
            dma((2,)),
            dma((2,)),
        ],
        compiler_params=pltpu.CompilerParams(
            collective_id=0, has_side_effects=True, vmem_limit_bytes=24 * 1024 * 1024
        ),
        name="gather",
    )(*(
        pltpu.with_memory_space_constraint(x, pltpu.HBM)
        for x in (image, weight, bias.reshape(1, o), cotangent)
    ))
    grad_weight, grad_bias, output = pl.pallas_call(
        functools.partial(finish_kernel, n_f, n_s),
        out_shape=(
            jax.ShapeDtypeStruct((3, 3, o, depth), jnp.float32),
            jax.ShapeDtypeStruct((1, o), jnp.float32),
            jax.ShapeDtypeStruct((1, n_f * o, cols // n_in), jnp.bfloat16),
        ),
        in_specs=[vmem] * 5,
        out_specs=(any_space, vmem, any_space),
        scratch_shapes=[
            pltpu.VMEM((9, o, depth), jnp.float32),
            dma((9,)),
            dma(()),
        ],
        compiler_params=pltpu.CompilerParams(vmem_limit_bytes=20 * 1024 * 1024),
        name="finish",
    )(*between)
    return (output, grad_weight, grad_bias.reshape(o))


def solution(mesh):
    placed = (
        P(("groups", "sp", "filt"), None, "in"),
        P(None, None, "filt", None),
        P("filt"),
        P(("groups", "sp"), "filt", None),
    )
    return jax.shard_map(
        on_device,
        mesh=mesh,
        in_specs=placed,
        out_specs=(
            P(("groups", "sp", "filt"), None, "in"),
            P("groups", None, "filt", "in"),
            P(("groups", "filt")),
        ),
        check_vma=False,
    )
```

```python
import functools

import jax
import jax.numpy as jnp
from jax import lax
from jax.experimental import pallas as pl
from jax.experimental.pallas import tpu as pltpu
from jax.sharding import PartitionSpec as P

MESH = pl.DeviceIdType.MESH
NT = (((1,), (1,)), ((), ()))


def shift_cols(value, by):
    cols = value.shape[1]
    col = lax.broadcasted_iota(jnp.int32, value.shape, 1)
    if by < 0:
        return jnp.where(col == 0, 0.0, pltpu.roll(value, 1, 1))
    return jnp.where(col == cols - 1, 0.0, pltpu.roll(value, cols - 1, 1))


def lanes(q, cols, count=1):
    return pl.ds(pl.multiple_of(q * cols, cols), count * cols)


def store_shifts(grads, gb_own, place, grad):
    wide = grad.astype(jnp.float32)
    width = gb_own.shape[1]
    gb_own[...] += sum(wide[:, k:k + width] for k in range(0, wide.shape[1], width))
    grads[0, :, place] = shift_cols(wide, 1).astype(jnp.bfloat16)
    grads[2, :, place] = shift_cols(wide, -1).astype(jnp.bfloat16)


def rows_tap(rows, grads, a, start, count):
    cols, depth = rows.shape[1], rows.shape[2]
    o = grads.shape[1]
    window = rows[pl.ds(start + a, count)].reshape(count * cols, depth)
    left = grads[:, :, lanes(start, cols, count)].reshape(3 * o, count * cols)
    return jnp.dot(left, window, preferred_element_type=jnp.float32).reshape(3, o, depth)


def late_row(block, n_f):
    return block * n_f + jnp.where(block > 0, 0, n_f - 1)


def early_row(block, n_f):
    return block * n_f + jnp.where(block > 0, 1, 0)


def gather_kernel(
    n_f, n_s,
    image, weight, bias_in, cotangent,
    rows, grads, gw_own, gb_own, out,
    w, bias, cot, part, peer, act,
    load_sem, ready_z, ready_x, row_send, row_recv, x_send, sum_send, sum_recv,
    g_send, g_recv, h_send, h_recv, out_send, out_recv, cot_send, cot_recv,
):
    p, s, c = lax.axis_index("filt"), lax.axis_index("sp"), lax.axis_index("in")
    sibling = 1 - c
    cols, depth = rows.shape[1], rows.shape[2]
    o = w.shape[2]
    half_c = out.shape[1]
    total = n_f * n_s
    first = s * n_f
    last = n_f - 1
    x_peers = [lax.rem(s + d, n_s) for d in range(1, n_s)]
    pair = n_s == 2
    other = 1 - s
    low = p < n_f // 2
    dist = jnp.where(low, p, last - p)
    early = (low & (s == 0)) | ((p >= n_f // 2) & (s > 0))
    late = (low & (s > 0)) | ((p >= n_f // 2) & (s == 0))
    bound = jnp.where(s == 0, n_f, -1)
    own_bound = jnp.where(s == 0, last, 0)
    bound_at = jnp.maximum(last - dist, jnp.maximum(dist + 1, 2))
    near = n_f // 2

    load_row = pltpu.make_async_copy(image.at[0], rows.at[1 + first + p], load_sem.at[0])
    load_w = pltpu.make_async_copy(
        weight.at[:, :, :, pl.ds(pl.multiple_of(c * depth, depth), depth)], w, load_sem.at[1]
    )
    load_cot = pltpu.make_async_copy(cotangent, cot.at[pl.ds(1, n_f)], load_sem.at[2])
    load_bias = pltpu.make_async_copy(bias_in, bias, load_sem.at[3])
    barrier = pltpu.get_barrier_semaphore()

    @pl.when(p < last)
    def _():
        pl.semaphore_signal(barrier, 1, device_id={"filt": p + 1}, device_id_type=MESH)

    for peer_s in x_peers:
        @pl.when(peer_s > s)
        def _():
            pl.semaphore_signal(barrier, 1, device_id={"sp": peer_s}, device_id_type=MESH)

    pl.semaphore_signal(barrier, 1, device_id={"in": sibling}, device_id_type=MESH)
    pl.semaphore_wait(barrier, 1 + s + jnp.where(p > 0, 1, 0))

    piece = cols // 2

    def row_copy(q, h, way, where, send):
        slot = rows.at[1 + q, pl.ds(h * piece, piece)]
        return pltpu.make_async_remote_copy(
            src_ref=slot, dst_ref=slot, send_sem=send, recv_sem=row_recv.at[q, h],
            device_id={way: where}, device_id_type=MESH,
        )

    def to_right(q, h):
        return row_copy(q, h, "filt", p + 1, row_send.at[0, q, h])

    def to_left(q, h):
        return row_copy(q, h, "filt", p - 1, row_send.at[1, q, h])

    def to_x(q, h, d):
        return row_copy(first + q, h, "sp", x_peers[d], x_send.at[d, q, h])

    def wait_row(q, h):
        row_copy(q, h, "filt", p, row_send.at[0, 0, 0]).wait_recv()

    def crosses(q, h):
        return ((q > 0) & (q < last)) | (q == p) | (h == 0)

    def pass_on(q, h, right, left):
        if right:
            @pl.when(p < last)
            def _():
                to_right(first + q, h).start()
        if left:
            @pl.when(p > 0)
            def _():
                to_left(first + q, h).start()

        @pl.when(crosses(q, h))
        def _():
            for d in range(n_s - 1):
                to_x(q, h, d).start()

    def own_copy(h, way, where, send):
        place = pl.ds(h * piece, piece)
        return pltpu.make_async_remote_copy(
            src_ref=image.at[0, place], dst_ref=rows.at[1 + first + p, place],
            send_sem=send, recv_sem=row_recv.at[first + p, h],
            device_id={way: where}, device_id_type=MESH,
        )

    def own_to_x(up):
        for d in range(n_s - 1):
            @pl.when((x_peers[d] > s) if up else (x_peers[d] < s))
            def _():
                for h in range(2):
                    own_copy(h, "sp", x_peers[d], x_send.at[d, p, h]).start()

    @pl.when(p > 0)
    def _():
        for h in range(2):
            own_copy(h, "filt", p - 1, row_send.at[1, first + p, h]).start()
        pl.semaphore_signal(ready_z, 1, device_id={"filt": p - 1}, device_id_type=MESH)

    own_to_x(False)
    for peer_s in x_peers:
        @pl.when(peer_s < s)
        def _():
            pl.semaphore_signal(ready_x, 1, device_id={"sp": peer_s}, device_id_type=MESH)

    load_row.start()
    load_w.start()
    load_cot.start()
    load_bias.start()

    @pl.when(p < last)
    def _():
        pl.semaphore_wait(ready_z, 1)
        for h in range(2):
            own_copy(h, "filt", p + 1, row_send.at[0, first + p, h]).start()

    @pl.when(s < n_s - 1)
    def _():
        pl.semaphore_wait(ready_x, n_s - 1 - s)

    own_to_x(True)
    load_row.wait()

    zero = jnp.zeros((cols, depth), rows.dtype)
    rows[0] = zero
    rows[total + 1] = zero

    @pl.loop(0, n_f + 2)
    def _(r):
        part[r] = jnp.zeros((o, cols), jnp.float32)

    load_w.wait()

    if pair:
        @pl.loop(0, 9)
        def _(k):
            gw_own[k] = jnp.zeros((o, depth), jnp.float32)

    gb_own[...] = jnp.zeros(gb_own.shape, jnp.float32)

    def add_tap(q, a, r):
        sums = lax.dot_general(
            w[a].reshape(3 * o, depth), rows[1 + q], NT, preferred_element_type=jnp.float32
        )
        part[r + 1] += shift_cols(sums[:o], -1) + sums[o:2 * o] + shift_cols(sums[2 * o:], 1)

    def add_row(q):
        sums = lax.dot_general(
            w[...].reshape(9 * o, depth), rows[1 + first + q], NT, preferred_element_type=jnp.float32
        )
        for a in range(3):
            left, middle, right = (sums[(3 * a + b) * o:(3 * a + b + 1) * o] for b in range(3))
            part[q - a + 2] += shift_cols(left, -1) + middle + shift_cols(right, 1)

    def sum_copy(r):
        return pltpu.make_async_remote_copy(
            src_ref=part.at[r + 1], dst_ref=peer.at[r + 1],
            send_sem=sum_send.at[r + 1], recv_sem=sum_recv.at[r + 1],
            device_id={"in": sibling}, device_id_type=MESH,
        )

    def out_copy(r):
        return pltpu.make_async_remote_copy(
            src_ref=act.at[r, :, pl.ds(pl.multiple_of(c * half_c, half_c), half_c)],
            dst_ref=out.at[pl.ds(pl.multiple_of(p * o, o), o), :],
            send_sem=out_send.at[r], recv_sem=out_recv.at[p],
            device_id={"filt": r}, device_id_type=MESH,
        )

    own_out = pltpu.make_async_copy(
        act.at[p, :, pl.ds(pl.multiple_of(c * half_c, half_c), half_c)],
        out.at[pl.ds(pl.multiple_of(p * o, o), o), :],
        load_sem.at[0],
    )

    half_o = o // 2

    def g_half(q, core):
        return grads.at[1, pl.ds(pl.multiple_of(core * half_o, half_o), half_o), lanes(q, cols)]

    def g_copy(q, d):
        place = g_half(q, c)
        return pltpu.make_async_remote_copy(
            src_ref=place, dst_ref=place, send_sem=g_send.at[d, q], recv_sem=g_recv.at[q],
            device_id={"sp": x_peers[d]}, device_id_type=MESH,
        )

    def h_copy(q, core):
        place = g_half(q, core)
        return pltpu.make_async_remote_copy(
            src_ref=place, dst_ref=place, send_sem=h_send.at[q], recv_sem=h_recv.at[q],
            device_id={"in": sibling}, device_id_type=MESH,
        )

    def half(place, core):
        return place.at[pl.ds(pl.multiple_of(core * half_o, half_o), half_o)]

    def cot_copy():
        return pltpu.make_async_remote_copy(
            src_ref=half(cotangent.at[own_bound], c),
            dst_ref=half(cot.at[jnp.where(s == 0, 0, n_f + 1)], c),
            send_sem=cot_send.at[0], recv_sem=cot_recv.at[0],
            device_id={"sp": other}, device_id_type=MESH,
        )

    def cot_share(core):
        place = half(cot.at[bound + 1], core)
        return pltpu.make_async_remote_copy(
            src_ref=place, dst_ref=place, send_sem=cot_send.at[1], recv_sem=cot_recv.at[1],
            device_id={"in": sibling}, device_id_type=MESH,
        )

    def done_at(r):
        low = jnp.where(s == 0, jnp.maximum(p, 1), jnp.maximum(p, n_f - p))
        high = jnp.where(
            s == n_s - 1, jnp.maximum(last - p, 1), jnp.maximum(last - p, p + 1)
        )
        return jnp.where(r == 0, low, jnp.where(r == last, high, jnp.abs(r - p) + 1))

    def finished_at(r):
        if not pair:
            return done_at(r)
        return jnp.where(
            (dist > 0) & (done_at(r) < last - dist), done_at(r) + 1, done_at(r)
        )

    def sends_grad(r):
        return early | (r != own_bound) if pair else r >= 0

    def activate(r):
        sum_copy(r).wait_recv()
        bias_all = jnp.broadcast_to(bias[...], (cols, o)).T
        shifted = part[r + 1] + peer[r + 1] + bias_all
        sig = jax.nn.sigmoid(shifted)
        slope = sig * (1.0 + shifted * (1.0 - sig))
        grad = (cot[r + 1].astype(jnp.float32) * slope).astype(jnp.bfloat16)
        grads[1, :, lanes(first + r, cols)] = grad
        return grad, (shifted * sig).astype(jnp.bfloat16)

    def finish(r):
        grad, value = activate(r)
        act[r] = value

        @pl.when(sends_grad(r))
        def _():
            for d in range(n_s - 1):
                g_copy(first + r, d).start()

        send_out(r)
        store_shifts(grads, gb_own, lanes(first + r, cols), grad)

    def finish_bound():
        grad, _ = activate(bound)
        store_shifts(grads, gb_own, lanes(first + bound, cols), grad)

    def send_out(r):
        @pl.when(r == p)
        def _():
            own_out.start()

        @pl.when(r != p)
        def _():
            out_copy(r).start()

    add_row(p)
    load_cot.wait()
    load_bias.wait()

    def relay(t):
        @pl.when(t == p + 1)
        def _():
            for block in x_peers:
                wait_row(block * n_f, 1)

                @pl.when(p < last)
                def _():
                    to_right(block * n_f, 1).start()

        @pl.when(t == n_f - p)
        def _():
            for block in x_peers:
                wait_row(block * n_f + last, 1)

                @pl.when(p > 0)
                def _():
                    to_left(block * n_f + last, 1).start()

    def settle(t):
        @pl.when(t == p + 1)
        def _():
            for block in x_peers:
                wait_row(block * n_f, 0)

        @pl.when(t == n_f - p)
        def _():
            for block in x_peers:
                wait_row(block * n_f + last, 0)

    def add_edges(t):
        if pair:
            tap = jnp.where(s == 0, 2, 0)
            edge = jnp.where(s == 0, first + n_f, first - 1)
            after = jnp.where(s == 0, first + n_f + 1, first - 2)

            @pl.when(t == jnp.where(early, dist + 1, n_f - dist))
            def _():
                add_tap(edge, tap, own_bound)

            @pl.when(early & (t == dist + 1))
            def _():
                add_tap(edge, 1, bound)

            @pl.when(early & (t == jnp.maximum(dist + 1, 2)))
            def _():
                for h in range(2):
                    wait_row(after, h)
                add_tap(after, tap, bound)

            return

        @pl.when((t == p + 1) & (s < n_s - 1))
        def _():
            add_tap(first + n_f, 2, last)

        @pl.when((t == n_f - p) & (s > 0))
        def _():
            add_tap(first - 1, 0, 0)

    def start_sums(t):
        @pl.loop(0, n_f)
        def _(r):
            @pl.when(done_at(r) == t)
            def _():
                sum_copy(r).start()

        if pair:
            @pl.when(early & (t == bound_at))
            def _():
                sum_copy(bound).start()

    def finish_rows(t):
        @pl.loop(0, n_f)
        def _(r):
            @pl.when(finished_at(r) == t)
            def _():
                finish(r)

    own_start = early_row(s, n_f)

    def own_rows(a):
        gw_own[3 * a:3 * a + 3] = rows_tap(rows, grads, a, own_start, n_f - 1)

    def add_rows(a, start, count):
        gw_own[3 * a:3 * a + 3] += rows_tap(rows, grads, a, start, count)

    def share_grad(q):
        g_copy(q, 0).wait_recv()
        h_copy(q, c).start()

    def take_grad(q):
        h_copy(q, sibling).wait_recv()
        place = lanes(q, cols)
        store_shifts(grads, gb_own, place, grads[1, :, place])

    def add_all(start, count):
        for a in range(3):
            add_rows(a, start, count)

    def near_rows():
        @pl.when(early)
        def _():
            add_all(first + jnp.where(low, 0, n_f - near), near)

        @pl.when(late)
        def _():
            add_all(first + jnp.where(low, 1, n_f - near), near - 1)

    def far_rows():
        add_all(first + jnp.where(low, near, 0), n_f - near)

    def tail_of_pair():
        def place(k):
            return other * n_f + jnp.where(low, k, last - k)

        @pl.when(early)
        def _():
            cot_copy().wait_recv()
            cot_share(c).start()

        @pl.when(late)
        def _():
            share_grad(place(0))

        @pl.when(dist == 0)
        def _():
            far_rows()

        @pl.loop(1, near)
        def _(k):
            share_grad(place(k))

        @pl.when(early)
        def _():
            cot_share(sibling).wait_recv()
            finish_bound()

        relay(n_f)
        settle(n_f)

        @pl.when(late)
        def _():
            add_edges(n_f)
            start_sums(n_f)
            take_grad(place(0))
            for h in range(2):
                wait_row(place(1), h)

        @pl.loop(1, near)
        def _(k):
            take_grad(place(k))

        @pl.loop(2, last)
        def _(k):
            for h in range(2):
                wait_row(place(k), h)

        add_all(other * n_f + jnp.where(low, 0, n_f - near), near)

        @pl.when(late)
        def _():
            finish_rows(n_f)

        @pl.loop(near, n_f)
        def _(k):
            share_grad(place(k))

        @pl.when(late)
        def _():
            add_all(first + own_bound, 1)

        @pl.loop(near, n_f)
        def _(k):
            take_grad(place(k))

    def tail_of_many():
        relay(n_f)
        settle(n_f)
        add_edges(n_f)
        start_sums(n_f)
        finish_rows(n_f)
        for a in range(3):
            own_rows(a)

        for block in x_peers:
            start = early_row(block, n_f)

            @pl.loop(1, last)
            def _(q):
                for h in range(2):
                    wait_row(block * n_f + q, h)

            @pl.loop(0, n_f - 1)
            def _(q):
                share_grad(start + q)

            @pl.loop(0, n_f - 1)
            def _(q):
                take_grad(start + q)

            for a in range(3):
                add_rows(a, start, n_f - 1)


        for block in x_peers:
            share_grad(late_row(block, n_f))
            take_grad(late_row(block, n_f))

    @pl.loop(1, n_f)
    def _(t):
        for h in range(2):
            @pl.when(p - t >= 0)
            def _():
                wait_row(first + p - t, h)
                pass_on(p - t, h, True, False)

            @pl.when(p + t < n_f)
            def _():
                wait_row(first + p + t, h)
                pass_on(p + t, h, False, True)

        relay(t)

        if pair:
            @pl.when((t == last) & (dist > 0))
            def _():
                near_rows()
                far_rows()

        settle(t)

        @pl.when(p - t >= 0)
        def _():
            add_row(p - t)

        @pl.when(p + t < n_f)
        def _():
            add_row(p + t)

        add_edges(t)
        start_sums(t)

        if pair:
            @pl.when(late & (t == n_f - 2))
            def _():
                cot_copy().start()

        finish_rows(t)

        if pair:
            @pl.when((t == n_f - 2) & (dist == 0))
            def _():
                near_rows()

    if pair:
        tail_of_pair()
    else:
        tail_of_many()

    @pl.loop(0, n_f)
    def _(r):
        sum_copy(r).wait_send()

        @pl.when(r == p)
        def _():
            own_out.wait()

        @pl.when(r != p)
        def _():
            out_copy(r).wait_send()
            pltpu.make_async_remote_copy(
                src_ref=act.at[r, :, pl.ds(0, half_c)],
                dst_ref=out.at[pl.ds(pl.multiple_of(r * o, o), o), :],
                send_sem=out_send.at[r], recv_sem=out_recv.at[r],
                device_id={"filt": r}, device_id_type=MESH,
            ).wait_recv()

        for d in range(n_s - 1):
            @pl.when(sends_grad(r))
            def _():
                g_copy(first + r, d).wait_send()

            for h in range(2):
                @pl.when(crosses(r, h))
                def _():
                    to_x(r, h, d).wait_send()

        @pl.when((r <= p) & (p < last))
        def _():
            for h in range(2):
                to_right(first + r, h).wait_send()

        @pl.when((r >= p) & (p > 0))
        def _():
            for h in range(2):
                to_left(first + r, h).wait_send()

    for block in x_peers:
        @pl.loop(0, n_f)
        def _(q):
            if pair:
                @pl.when(late | (q != jnp.where(low, 0, last)))
                def _():
                    h_copy(block * n_f + q, c).wait_send()
            else:
                h_copy(block * n_f + q, c).wait_send()

        @pl.when(p < last)
        def _():
            to_right(block * n_f, 1).wait_send()

        @pl.when(p > 0)
        def _():
            to_left(block * n_f + last, 1).wait_send()

    if pair:
        @pl.when(early)
        def _():
            sum_copy(bound).wait_send()
            cot_share(c).wait_send()

        @pl.when(late)
        def _():
            cot_copy().wait_send()


def finish_kernel(n_f, n_s, rows, grads, gw_own, gb_own, out_in, gw, gb, out, total, sem, out_sem):
    cols = rows.shape[1]
    out_copy = pltpu.make_async_copy(out_in, out.at[0], out_sem)
    out_copy.start()

    if n_s == 2:
        p, s = lax.axis_index("filt"), lax.axis_index("sp")
        late = [((1 - s) * n_f + jnp.where(p < n_f // 2, n_f // 2, 0), n_f - n_f // 2)]
    else:
        late = [(n_f - 1, 2)] + [(block * n_f, 1) for block in range(2, n_s)]

    def gw_copy(k):
        return pltpu.make_async_copy(total.at[k], gw.at[k // 3, k % 3], sem.at[k])

    gb[...] = jnp.sum(gb_own[...].T, axis=0, keepdims=True)

    for a in range(3):
        value = gw_own[3 * a:3 * a + 3]
        for start, count in late:
            value = value + rows_tap(rows, grads, a, start, count)
        for b in range(3):
            total[3 * a + b] = value[b]
            gw_copy(3 * a + b).start()

    for k in range(9):
        gw_copy(k).wait()

    out_copy.wait()


def on_device(image, weight, bias, cotangent):
    n_f, n_s, n_in = (lax.axis_size(name) for name in ("filt", "sp", "in"))
    row_count, o, cols = cotangent.shape
    depth = image.shape[2]
    total = n_f * n_s
    any_space = pl.BlockSpec(memory_space=pl.ANY)
    vmem = pl.BlockSpec(memory_space=pltpu.VMEM)
    hbm = pl.BlockSpec(memory_space=pltpu.HBM)
    dma = pltpu.SemaphoreType.DMA
    between = pl.pallas_call(
        functools.partial(gather_kernel, n_f, n_s),
        out_shape=(
            pltpu.VMEM((total + 2, cols, depth), jnp.bfloat16),
            pltpu.VMEM((3, o, total * cols), jnp.bfloat16),
            pltpu.VMEM((9, o, depth), jnp.float32),
            pltpu.VMEM((o, 128), jnp.float32),
            pltpu.VMEM((n_f * o, cols // n_in), jnp.bfloat16),
        ),
        in_specs=[hbm, hbm, hbm, hbm],
        out_specs=(vmem,) * 5,
        scratch_shapes=[
            pltpu.VMEM((3, 3, o, depth), jnp.bfloat16),
            pltpu.VMEM((1, o), jnp.float32),
            pltpu.VMEM((n_f + 2, o, cols), jnp.bfloat16),
            pltpu.VMEM((n_f + 2, o, cols), jnp.float32),
            pltpu.VMEM((n_f + 2, o, cols), jnp.float32),
            pltpu.VMEM((n_f, o, cols), jnp.bfloat16),
            dma((4,)),
            pltpu.SemaphoreType.REGULAR,
            pltpu.SemaphoreType.REGULAR,
            dma((2, total, 2)),
            dma((total, 2)),
            dma((n_s - 1, n_f, 2)),
            dma((n_f + 2,)),
            dma((n_f + 2,)),
            dma((n_s - 1, total)),
            dma((total,)),
            dma((total,)),
            dma((total,)),
            dma((n_f,)),
            dma((n_f,)),
            dma((2,)),
            dma((2,)),
        ],
        compiler_params=pltpu.CompilerParams(
            collective_id=0, has_side_effects=True, vmem_limit_bytes=24 * 1024 * 1024
        ),
        name="gather",
    )(*(
        pltpu.with_memory_space_constraint(x, pltpu.HBM)
        for x in (image, weight, bias.reshape(1, o), cotangent)
    ))
    grad_weight, grad_bias, output = pl.pallas_call(
        functools.partial(finish_kernel, n_f, n_s),
        out_shape=(
            jax.ShapeDtypeStruct((3, 3, o, depth), jnp.float32),
            jax.ShapeDtypeStruct((1, o), jnp.float32),
            jax.ShapeDtypeStruct((1, n_f * o, cols // n_in), jnp.bfloat16),
        ),
        in_specs=[vmem] * 5,
        out_specs=(any_space, vmem, any_space),
        scratch_shapes=[
            pltpu.VMEM((9, o, depth), jnp.float32),
            dma((9,)),
            dma(()),
        ],
        compiler_params=pltpu.CompilerParams(vmem_limit_bytes=20 * 1024 * 1024),
        name="finish",
    )(*between)
    return (output, grad_weight, grad_bias.reshape(o))


def solution(mesh):
    placed = (
        P(("groups", "sp", "filt"), None, "in"),
        P(None, None, "filt", None),
        P("filt"),
        P(("groups", "sp"), "filt", None),
    )
    return jax.shard_map(
        on_device,
        mesh=mesh,
        in_specs=placed,
        out_specs=(
            P(("groups", "sp", "filt"), None, "in"),
            P("groups", None, "filt", "in"),
            P(("groups", "filt")),
        ),
        check_vma=False,
    )
```

```python
import functools

import jax
import jax.numpy as jnp
from jax import lax
from jax.experimental import pallas as pl
from jax.experimental.pallas import tpu as pltpu
from jax.sharding import PartitionSpec as P

MESH = pl.DeviceIdType.MESH
NT = (((1,), (1,)), ((), ()))


def shift_cols(value, by):
    cols = value.shape[1]
    col = lax.broadcasted_iota(jnp.int32, value.shape, 1)
    if by < 0:
        return jnp.where(col == 0, 0.0, pltpu.roll(value, 1, 1))
    return jnp.where(col == cols - 1, 0.0, pltpu.roll(value, cols - 1, 1))


def lanes(q, cols, count=1):
    return pl.ds(pl.multiple_of(q * cols, cols), count * cols)


def store_shifts(grads, gb_own, place, grad):
    wide = grad.astype(jnp.float32)
    width = gb_own.shape[1]
    gb_own[...] += sum(wide[:, k:k + width] for k in range(0, wide.shape[1], width))
    grads[0, :, place] = shift_cols(wide, 1).astype(jnp.bfloat16)
    grads[2, :, place] = shift_cols(wide, -1).astype(jnp.bfloat16)


def rows_tap(rows, grads, a, start, count):
    cols, depth = rows.shape[1], rows.shape[2]
    o = grads.shape[1]
    window = rows[pl.ds(start + a, count)].reshape(count * cols, depth)
    left = grads[:, :, lanes(start, cols, count)].reshape(3 * o, count * cols)
    return jnp.dot(left, window, preferred_element_type=jnp.float32).reshape(3, o, depth)


def late_row(block, n_f):
    return block * n_f + jnp.where(block > 0, 0, n_f - 1)


def early_row(block, n_f):
    return block * n_f + jnp.where(block > 0, 1, 0)


def gather_kernel(
    n_f, n_s,
    image, weight, bias_in, cotangent,
    rows, grads, gw_own, gb_own, out,
    w, bias, cot, part, peer, act,
    load_sem, ready_z, ready_x, row_send, row_recv, x_send, sum_send, sum_recv,
    g_send, g_recv, h_send, h_recv, out_send, out_recv, cot_send, cot_recv,
):
    p, s, c = lax.axis_index("filt"), lax.axis_index("sp"), lax.axis_index("in")
    sibling = 1 - c
    cols, depth = rows.shape[1], rows.shape[2]
    o = w.shape[2]
    half_c = out.shape[1]
    total = n_f * n_s
    first = s * n_f
    last = n_f - 1
    x_peers = [lax.rem(s + d, n_s) for d in range(1, n_s)]
    pair = n_s == 2
    other = 1 - s
    low = p < n_f // 2
    dist = jnp.where(low, p, last - p)
    early = (low & (s == 0)) | ((p >= n_f // 2) & (s > 0))
    late = (low & (s > 0)) | ((p >= n_f // 2) & (s == 0))
    bound = jnp.where(s == 0, n_f, -1)
    own_bound = jnp.where(s == 0, last, 0)
    bound_at = jnp.maximum(last - dist, jnp.maximum(dist + 1, 2))
    near = n_f // 2

    load_row = pltpu.make_async_copy(image.at[0], rows.at[1 + first + p], load_sem.at[0])
    load_w = pltpu.make_async_copy(
        weight.at[:, :, :, pl.ds(pl.multiple_of(c * depth, depth), depth)], w, load_sem.at[1]
    )
    load_cot = pltpu.make_async_copy(cotangent, cot.at[pl.ds(1, n_f)], load_sem.at[2])
    load_bias = pltpu.make_async_copy(bias_in, bias, load_sem.at[3])
    barrier = pltpu.get_barrier_semaphore()

    @pl.when(p < last)
    def _():
        pl.semaphore_signal(barrier, 1, device_id={"filt": p + 1}, device_id_type=MESH)

    for peer_s in x_peers:
        @pl.when(peer_s > s)
        def _():
            pl.semaphore_signal(barrier, 1, device_id={"sp": peer_s}, device_id_type=MESH)

    pl.semaphore_signal(barrier, 1, device_id={"in": sibling}, device_id_type=MESH)
    pl.semaphore_wait(barrier, 1 + s + jnp.where(p > 0, 1, 0))

    cut = cols * 3 // 8

    def span(h):
        return pl.ds(0, cut) if h == 0 else pl.ds(cut, cols - cut)

    def row_copy(q, h, way, where, send):
        slot = rows.at[1 + q, span(h)]
        return pltpu.make_async_remote_copy(
            src_ref=slot, dst_ref=slot, send_sem=send, recv_sem=row_recv.at[q, h],
            device_id={way: where}, device_id_type=MESH,
        )

    def to_right(q, h):
        return row_copy(q, h, "filt", p + 1, row_send.at[0, q, h])

    def to_left(q, h):
        return row_copy(q, h, "filt", p - 1, row_send.at[1, q, h])

    def to_x(q, h, d):
        return row_copy(first + q, h, "sp", x_peers[d], x_send.at[d, q, h])

    def wait_row(q, h):
        row_copy(q, h, "filt", p, row_send.at[0, 0, 0]).wait_recv()

    def crosses(q, h):
        return ((q > 0) & (q < last)) | (q == p) | (h == 0)

    def pass_on(q, h, right, left):
        if right:
            @pl.when(p < last)
            def _():
                to_right(first + q, h).start()
        if left:
            @pl.when(p > 0)
            def _():
                to_left(first + q, h).start()

        @pl.when(crosses(q, h))
        def _():
            for d in range(n_s - 1):
                to_x(q, h, d).start()

    def own_copy(h, way, where, send):
        place = span(h)
        return pltpu.make_async_remote_copy(
            src_ref=image.at[0, place], dst_ref=rows.at[1 + first + p, place],
            send_sem=send, recv_sem=row_recv.at[first + p, h],
            device_id={way: where}, device_id_type=MESH,
        )

    def own_to_x(up):
        for d in range(n_s - 1):
            @pl.when((x_peers[d] > s) if up else (x_peers[d] < s))
            def _():
                for h in range(2):
                    own_copy(h, "sp", x_peers[d], x_send.at[d, p, h]).start()

    @pl.when(p > 0)
    def _():
        for h in range(2):
            own_copy(h, "filt", p - 1, row_send.at[1, first + p, h]).start()
        pl.semaphore_signal(ready_z, 1, device_id={"filt": p - 1}, device_id_type=MESH)

    own_to_x(False)
    for peer_s in x_peers:
        @pl.when(peer_s < s)
        def _():
            pl.semaphore_signal(ready_x, 1, device_id={"sp": peer_s}, device_id_type=MESH)

    load_row.start()
    load_w.start()
    load_cot.start()
    load_bias.start()

    @pl.when(p < last)
    def _():
        pl.semaphore_wait(ready_z, 1)
        for h in range(2):
            own_copy(h, "filt", p + 1, row_send.at[0, first + p, h]).start()

    @pl.when(s < n_s - 1)
    def _():
        pl.semaphore_wait(ready_x, n_s - 1 - s)

    own_to_x(True)
    load_row.wait()

    zero = jnp.zeros((cols, depth), rows.dtype)
    rows[0] = zero
    rows[total + 1] = zero

    @pl.loop(0, n_f + 2)
    def _(r):
        part[r] = jnp.zeros((o, cols), jnp.float32)

    load_w.wait()

    if pair:
        @pl.loop(0, 9)
        def _(k):
            gw_own[k] = jnp.zeros((o, depth), jnp.float32)

    gb_own[...] = jnp.zeros(gb_own.shape, jnp.float32)

    def add_tap(q, a, r):
        sums = lax.dot_general(
            w[a].reshape(3 * o, depth), rows[1 + q], NT, preferred_element_type=jnp.float32
        )
        part[r + 1] += shift_cols(sums[:o], -1) + sums[o:2 * o] + shift_cols(sums[2 * o:], 1)

    def add_row(q):
        sums = lax.dot_general(
            w[...].reshape(9 * o, depth), rows[1 + first + q], NT, preferred_element_type=jnp.float32
        )
        for a in range(3):
            left, middle, right = (sums[(3 * a + b) * o:(3 * a + b + 1) * o] for b in range(3))
            part[q - a + 2] += shift_cols(left, -1) + middle + shift_cols(right, 1)

    def sum_copy(r):
        return pltpu.make_async_remote_copy(
            src_ref=part.at[r + 1], dst_ref=peer.at[r + 1],
            send_sem=sum_send.at[r + 1], recv_sem=sum_recv.at[r + 1],
            device_id={"in": sibling}, device_id_type=MESH,
        )

    def out_copy(r):
        return pltpu.make_async_remote_copy(
            src_ref=act.at[r, :, pl.ds(pl.multiple_of(c * half_c, half_c), half_c)],
            dst_ref=out.at[pl.ds(pl.multiple_of(p * o, o), o), :],
            send_sem=out_send.at[r], recv_sem=out_recv.at[p],
            device_id={"filt": r}, device_id_type=MESH,
        )

    own_out = pltpu.make_async_copy(
        act.at[p, :, pl.ds(pl.multiple_of(c * half_c, half_c), half_c)],
        out.at[pl.ds(pl.multiple_of(p * o, o), o), :],
        load_sem.at[0],
    )

    half_o = o // 2

    def g_half(q, core):
        return grads.at[1, pl.ds(pl.multiple_of(core * half_o, half_o), half_o), lanes(q, cols)]

    def g_copy(q, d):
        place = g_half(q, c)
        return pltpu.make_async_remote_copy(
            src_ref=place, dst_ref=place, send_sem=g_send.at[d, q], recv_sem=g_recv.at[q],
            device_id={"sp": x_peers[d]}, device_id_type=MESH,
        )

    def h_copy(q, core):
        place = g_half(q, core)
        return pltpu.make_async_remote_copy(
            src_ref=place, dst_ref=place, send_sem=h_send.at[q], recv_sem=h_recv.at[q],
            device_id={"in": sibling}, device_id_type=MESH,
        )

    def half(place, core):
        return place.at[pl.ds(pl.multiple_of(core * half_o, half_o), half_o)]

    def cot_copy():
        return pltpu.make_async_remote_copy(
            src_ref=half(cotangent.at[own_bound], c),
            dst_ref=half(cot.at[jnp.where(s == 0, 0, n_f + 1)], c),
            send_sem=cot_send.at[0], recv_sem=cot_recv.at[0],
            device_id={"sp": other}, device_id_type=MESH,
        )

    def cot_share(core):
        place = half(cot.at[bound + 1], core)
        return pltpu.make_async_remote_copy(
            src_ref=place, dst_ref=place, send_sem=cot_send.at[1], recv_sem=cot_recv.at[1],
            device_id={"in": sibling}, device_id_type=MESH,
        )

    def done_at(r):
        low = jnp.where(s == 0, jnp.maximum(p, 1), jnp.maximum(p, n_f - p))
        high = jnp.where(
            s == n_s - 1, jnp.maximum(last - p, 1), jnp.maximum(last - p, p + 1)
        )
        return jnp.where(r == 0, low, jnp.where(r == last, high, jnp.abs(r - p) + 1))

    def finished_at(r):
        if not pair:
            return done_at(r)
        return jnp.where(
            (dist > 0) & (done_at(r) < last - dist), done_at(r) + 1, done_at(r)
        )

    def sends_grad(r):
        return early | (r != own_bound) if pair else r >= 0

    def activate(r):
        sum_copy(r).wait_recv()
        bias_all = jnp.broadcast_to(bias[...], (cols, o)).T
        shifted = part[r + 1] + peer[r + 1] + bias_all
        sig = jax.nn.sigmoid(shifted)
        slope = sig * (1.0 + shifted * (1.0 - sig))
        grad = (cot[r + 1].astype(jnp.float32) * slope).astype(jnp.bfloat16)
        grads[1, :, lanes(first + r, cols)] = grad
        return grad, (shifted * sig).astype(jnp.bfloat16)

    def finish(r):
        grad, value = activate(r)
        act[r] = value

        @pl.when(sends_grad(r))
        def _():
            for d in range(n_s - 1):
                g_copy(first + r, d).start()

        send_out(r)
        store_shifts(grads, gb_own, lanes(first + r, cols), grad)

    def finish_bound():
        grad, _ = activate(bound)
        store_shifts(grads, gb_own, lanes(first + bound, cols), grad)

    def send_out(r):
        @pl.when(r == p)
        def _():
            own_out.start()

        @pl.when(r != p)
        def _():
            out_copy(r).start()

    add_row(p)
    load_cot.wait()
    load_bias.wait()

    def relay(t):
        @pl.when(t == p + 1)
        def _():
            for block in x_peers:
                wait_row(block * n_f, 1)

                @pl.when(p < last)
                def _():
                    to_right(block * n_f, 1).start()

        @pl.when(t == n_f - p)
        def _():
            for block in x_peers:
                wait_row(block * n_f + last, 1)

                @pl.when(p > 0)
                def _():
                    to_left(block * n_f + last, 1).start()

    def settle(t):
        @pl.when(t == p + 1)
        def _():
            for block in x_peers:
                wait_row(block * n_f, 0)

        @pl.when(t == n_f - p)
        def _():
            for block in x_peers:
                wait_row(block * n_f + last, 0)

    def add_edges(t):
        if pair:
            tap = jnp.where(s == 0, 2, 0)
            edge = jnp.where(s == 0, first + n_f, first - 1)
            after = jnp.where(s == 0, first + n_f + 1, first - 2)

            @pl.when(t == jnp.where(early, dist + 1, n_f - dist))
            def _():
                add_tap(edge, tap, own_bound)

            @pl.when(early & (t == dist + 1))
            def _():
                add_tap(edge, 1, bound)

            @pl.when(early & (t == jnp.maximum(dist + 1, 2)))
            def _():
                for h in range(2):
                    wait_row(after, h)
                add_tap(after, tap, bound)

            return

        @pl.when((t == p + 1) & (s < n_s - 1))
        def _():
            add_tap(first + n_f, 2, last)

        @pl.when((t == n_f - p) & (s > 0))
        def _():
            add_tap(first - 1, 0, 0)

    def start_sums(t):
        @pl.loop(0, n_f)
        def _(r):
            @pl.when(done_at(r) == t)
            def _():
                sum_copy(r).start()

        if pair:
            @pl.when(early & (t == bound_at))
            def _():
                sum_copy(bound).start()

    def finish_rows(t):
        @pl.loop(0, n_f)
        def _(r):
            @pl.when(finished_at(r) == t)
            def _():
                finish(r)

    own_start = early_row(s, n_f)

    def own_rows(a):
        gw_own[3 * a:3 * a + 3] = rows_tap(rows, grads, a, own_start, n_f - 1)

    def add_rows(a, start, count):
        gw_own[3 * a:3 * a + 3] += rows_tap(rows, grads, a, start, count)

    def share_grad(q):
        g_copy(q, 0).wait_recv()
        h_copy(q, c).start()

    def take_grad(q):
        h_copy(q, sibling).wait_recv()
        place = lanes(q, cols)
        store_shifts(grads, gb_own, place, grads[1, :, place])

    def add_all(start, count):
        for a in range(3):
            add_rows(a, start, count)

    def near_rows():
        @pl.when(early)
        def _():
            add_all(first + jnp.where(low, 0, n_f - near), near)

        @pl.when(late)
        def _():
            add_all(first + jnp.where(low, 1, n_f - near), near - 1)

    def far_rows():
        add_all(first + jnp.where(low, near, 0), n_f - near)

    def tail_of_pair():
        def place(k):
            return other * n_f + jnp.where(low, k, last - k)

        @pl.when(early)
        def _():
            cot_copy().wait_recv()
            cot_share(c).start()

        @pl.when(late)
        def _():
            share_grad(place(0))

        @pl.when(dist == 0)
        def _():
            far_rows()

        @pl.loop(1, near)
        def _(k):
            share_grad(place(k))

        @pl.when(early)
        def _():
            cot_share(sibling).wait_recv()
            finish_bound()

        relay(n_f)
        settle(n_f)

        @pl.when(late)
        def _():
            add_edges(n_f)
            start_sums(n_f)
            take_grad(place(0))
            for h in range(2):
                wait_row(place(1), h)

        @pl.loop(1, near)
        def _(k):
            take_grad(place(k))

        @pl.loop(2, last)
        def _(k):
            for h in range(2):
                wait_row(place(k), h)

        add_all(other * n_f + jnp.where(low, 0, n_f - near), near)

        @pl.when(late)
        def _():
            finish_rows(n_f)

        @pl.loop(near, n_f)
        def _(k):
            share_grad(place(k))

        @pl.when(late)
        def _():
            add_all(first + own_bound, 1)

        @pl.loop(near, n_f)
        def _(k):
            take_grad(place(k))

    def tail_of_many():
        relay(n_f)
        settle(n_f)
        add_edges(n_f)
        start_sums(n_f)
        finish_rows(n_f)
        for a in range(3):
            own_rows(a)

        for block in x_peers:
            start = early_row(block, n_f)

            @pl.loop(1, last)
            def _(q):
                for h in range(2):
                    wait_row(block * n_f + q, h)

            @pl.loop(0, n_f - 1)
            def _(q):
                share_grad(start + q)

            @pl.loop(0, n_f - 1)
            def _(q):
                take_grad(start + q)

            for a in range(3):
                add_rows(a, start, n_f - 1)


        for block in x_peers:
            share_grad(late_row(block, n_f))
            take_grad(late_row(block, n_f))

    @pl.loop(1, n_f)
    def _(t):
        for h in range(2):
            @pl.when(p - t >= 0)
            def _():
                wait_row(first + p - t, h)
                pass_on(p - t, h, True, False)

            @pl.when(p + t < n_f)
            def _():
                wait_row(first + p + t, h)
                pass_on(p + t, h, False, True)

        relay(t)

        if pair:
            @pl.when((t == last) & (dist > 0))
            def _():
                near_rows()
                far_rows()

        settle(t)

        @pl.when(p - t >= 0)
        def _():
            add_row(p - t)

        @pl.when(p + t < n_f)
        def _():
            add_row(p + t)

        add_edges(t)
        start_sums(t)

        if pair:
            @pl.when(late & (t == n_f - 2))
            def _():
                cot_copy().start()

        finish_rows(t)

        if pair:
            @pl.when((t == n_f - 2) & (dist == 0))
            def _():
                near_rows()

    if pair:
        tail_of_pair()
    else:
        tail_of_many()

    @pl.loop(0, n_f)
    def _(r):
        sum_copy(r).wait_send()

        @pl.when(r == p)
        def _():
            own_out.wait()

        @pl.when(r != p)
        def _():
            out_copy(r).wait_send()
            pltpu.make_async_remote_copy(
                src_ref=act.at[r, :, pl.ds(0, half_c)],
                dst_ref=out.at[pl.ds(pl.multiple_of(r * o, o), o), :],
                send_sem=out_send.at[r], recv_sem=out_recv.at[r],
                device_id={"filt": r}, device_id_type=MESH,
            ).wait_recv()

        for d in range(n_s - 1):
            @pl.when(sends_grad(r))
            def _():
                g_copy(first + r, d).wait_send()

            for h in range(2):
                @pl.when(crosses(r, h))
                def _():
                    to_x(r, h, d).wait_send()

        @pl.when((r <= p) & (p < last))
        def _():
            for h in range(2):
                to_right(first + r, h).wait_send()

        @pl.when((r >= p) & (p > 0))
        def _():
            for h in range(2):
                to_left(first + r, h).wait_send()

    for block in x_peers:
        @pl.loop(0, n_f)
        def _(q):
            if pair:
                @pl.when(late | (q != jnp.where(low, 0, last)))
                def _():
                    h_copy(block * n_f + q, c).wait_send()
            else:
                h_copy(block * n_f + q, c).wait_send()

        @pl.when(p < last)
        def _():
            to_right(block * n_f, 1).wait_send()

        @pl.when(p > 0)
        def _():
            to_left(block * n_f + last, 1).wait_send()

    if pair:
        @pl.when(early)
        def _():
            sum_copy(bound).wait_send()
            cot_share(c).wait_send()

        @pl.when(late)
        def _():
            cot_copy().wait_send()


def finish_kernel(n_f, n_s, rows, grads, gw_own, gb_own, out_in, gw, gb, out, total, sem, out_sem):
    cols = rows.shape[1]
    out_copy = pltpu.make_async_copy(out_in, out.at[0], out_sem)
    out_copy.start()

    if n_s == 2:
        p, s = lax.axis_index("filt"), lax.axis_index("sp")
        late = [((1 - s) * n_f + jnp.where(p < n_f // 2, n_f // 2, 0), n_f - n_f // 2)]
    else:
        late = [(n_f - 1, 2)] + [(block * n_f, 1) for block in range(2, n_s)]

    def gw_copy(k):
        return pltpu.make_async_copy(total.at[k], gw.at[k // 3, k % 3], sem.at[k])

    for a in range(3):
        value = gw_own[3 * a:3 * a + 3]
        for start, count in late:
            value = value + rows_tap(rows, grads, a, start, count)
        for b in range(3):
            total[3 * a + b] = value[b]
            gw_copy(3 * a + b).start()

    gb[...] = jnp.sum(gb_own[...].T, axis=0, keepdims=True)

    for k in range(9):
        gw_copy(k).wait()

    out_copy.wait()


def on_device(image, weight, bias, cotangent):
    n_f, n_s, n_in = (lax.axis_size(name) for name in ("filt", "sp", "in"))
    row_count, o, cols = cotangent.shape
    depth = image.shape[2]
    total = n_f * n_s
    any_space = pl.BlockSpec(memory_space=pl.ANY)
    vmem = pl.BlockSpec(memory_space=pltpu.VMEM)
    hbm = pl.BlockSpec(memory_space=pltpu.HBM)
    dma = pltpu.SemaphoreType.DMA
    between = pl.pallas_call(
        functools.partial(gather_kernel, n_f, n_s),
        out_shape=(
            pltpu.VMEM((total + 2, cols, depth), jnp.bfloat16),
            pltpu.VMEM((3, o, total * cols), jnp.bfloat16),
            pltpu.VMEM((9, o, depth), jnp.float32),
            pltpu.VMEM((o, 128), jnp.float32),
            pltpu.VMEM((n_f * o, cols // n_in), jnp.bfloat16),
        ),
        in_specs=[hbm, hbm, hbm, hbm],
        out_specs=(vmem,) * 5,
        scratch_shapes=[
            pltpu.VMEM((3, 3, o, depth), jnp.bfloat16),
            pltpu.VMEM((1, o), jnp.float32),
            pltpu.VMEM((n_f + 2, o, cols), jnp.bfloat16),
            pltpu.VMEM((n_f + 2, o, cols), jnp.float32),
            pltpu.VMEM((n_f + 2, o, cols), jnp.float32),
            pltpu.VMEM((n_f, o, cols), jnp.bfloat16),
            dma((4,)),
            pltpu.SemaphoreType.REGULAR,
            pltpu.SemaphoreType.REGULAR,
            dma((2, total, 2)),
            dma((total, 2)),
            dma((n_s - 1, n_f, 2)),
            dma((n_f + 2,)),
            dma((n_f + 2,)),
            dma((n_s - 1, total)),
            dma((total,)),
            dma((total,)),
            dma((total,)),
            dma((n_f,)),
            dma((n_f,)),
            dma((2,)),
            dma((2,)),
        ],
        compiler_params=pltpu.CompilerParams(
            collective_id=0, has_side_effects=True, vmem_limit_bytes=24 * 1024 * 1024
        ),
        name="gather",
    )(*(
        pltpu.with_memory_space_constraint(x, pltpu.HBM)
        for x in (image, weight, bias.reshape(1, o), cotangent)
    ))
    grad_weight, grad_bias, output = pl.pallas_call(
        functools.partial(finish_kernel, n_f, n_s),
        out_shape=(
            jax.ShapeDtypeStruct((3, 3, o, depth), jnp.float32),
            jax.ShapeDtypeStruct((1, o), jnp.float32),
            jax.ShapeDtypeStruct((1, n_f * o, cols // n_in), jnp.bfloat16),
        ),
        in_specs=[vmem] * 5,
        out_specs=(any_space, vmem, any_space),
        scratch_shapes=[
            pltpu.VMEM((9, o, depth), jnp.float32),
            dma((9,)),
            dma(()),
        ],
        compiler_params=pltpu.CompilerParams(vmem_limit_bytes=20 * 1024 * 1024),
        name="finish",
    )(*between)
    return (output, grad_weight, grad_bias.reshape(o))


def solution(mesh):
    placed = (
        P(("groups", "sp", "filt"), None, "in"),
        P(None, None, "filt", None),
        P("filt"),
        P(("groups", "sp"), "filt", None),
    )
    return jax.shard_map(
        on_device,
        mesh=mesh,
        in_specs=placed,
        out_specs=(
            P(("groups", "sp", "filt"), None, "in"),
            P("groups", None, "filt", "in"),
            P(("groups", "filt")),
        ),
        check_vma=False,
    )
```
